512 devices in a mesh: row: 16 (over z, core), col: 32 (over x, y).
Axes of the slice: x: 4, y: 8, z: 8, core: 2. Of those that a mesh axis runs over, the one named last changes fastest.
Arguments:
- source_embed: float32 [64, 16384], P('col', 'row'), may hold values from -40 to 40
- target_embed: float32 [64, 32768], P('row', 'col'), may hold values from -40 to 40
- source_mass: float32 [16384], P('row'), may hold values from -2 to 2
- target_mass: float32 [32768], P('col'), may hold values from -2 to 2
- tile_list: int32 [16, 32, 2, 12], P('row', 'col'), may hold values from -1 to 127, as said below
- tile_counts: int32 [16, 32], P('row', 'col'), may hold values from 4 to 12, as said below
Outputs:
- source_potential: float32 [16384], P('row')
- target_potential: float32 [32768], P('col')
The draws below stay inside these ranges and needn't reach their ends.
Inputs may be any that keep to these rules, and one draw needn't show every extreme that they name: `tile_list`: for the device at row index r and col index c, the slots below tile_counts[r, c] name distinct tiles whose row block lies in r * 4 to (r + 1) * 4 - 1 and whose column block lies in c * 4 to (c + 1) * 4 - 1; every row block and every column block of those ranges appears among them; the later slots hold -1 in both entries. `tile_counts`: some device has all 12 slots live.
All inputs are finite; a program needn't handle non-finite values.
Results may differ from the reference program's by a relative error of at most 0.0003.
Values sent between devices are 32-bit elements; how exact they have to be, the bound alone decides.
A program may use at most 64 MiB of HBM per device.

```python
import jax
import jax.numpy as jnp
import numpy as np
from jax import lax

DIM = 64
TILE = 256
ITERS = 3
SRC_DEV = 1024
TGT_DEV = 1024
NSRC = 16384
NTGT = 32768
MAXT = 12
N_ROW = 16
N_COL = 32


def support_lists(key):
    root_key = jax.random.fold_in(key, 7)
    row_blocks = SRC_DEV // TILE
    col_blocks = TGT_DEV // TILE
    pair_count = row_blocks * col_blocks
    basic = max(row_blocks, col_blocks)
    surplus = MAXT - basic
    devices = N_ROW * N_COL
    flags = np.ones(pair_count, np.int32)
    members = np.arange(basic)
    flags[members % row_blocks * col_blocks + members % col_blocks] = 0
    flag_table = jnp.asarray(flags)

    def pick_pairs(device_key):
        shuffled = jax.random.permutation(device_key, pair_count).astype(jnp.int32)
        ordering = jnp.argsort(flag_table[shuffled], stable=True)
        return shuffled[ordering][:MAXT]
    chosen = jax.vmap(pick_pairs)(jax.random.split(jax.random.fold_in(root_key, 1), devices))
    device_ids = jnp.arange(devices, dtype=jnp.int32)
    row_index = device_ids // N_COL
    col_index = device_ids % N_COL
    lower_half = col_index < N_COL // 2
    odd_row = row_index % 2 == 1
    heavy = lower_half != odd_row
    heavy_counts = basic + surplus // 2 + jax.random.randint(jax.random.fold_in(root_key, 2), (devices,), 0, surplus - surplus // 2 + 1).astype(jnp.int32)
    light_counts = basic + jax.random.randint(jax.random.fold_in(root_key, 4), (devices,), 0, surplus // 8 + 1).astype(jnp.int32)
    counted = jnp.where(heavy, heavy_counts, light_counts)
    busiest = jax.random.randint(jax.random.fold_in(root_key, 3), (), 0, devices)
    counted = jnp.where(device_ids == busiest, MAXT, counted).astype(jnp.int32)
    row_ids = row_index[:, None] * row_blocks + chosen // col_blocks
    col_ids = col_index[:, None] * col_blocks + chosen % col_blocks
    live_slots = jnp.arange(MAXT, dtype=jnp.int32)[None, :] < counted[:, None]
    row_ids = jnp.where(live_slots, row_ids, -1)
    col_ids = jnp.where(live_slots, col_ids, -1)
    listing = jnp.stack([row_ids, col_ids], axis=1).reshape(N_ROW, N_COL, 2, MAXT)
    return (listing.astype(jnp.int32), counted.reshape(N_ROW, N_COL))


def draw_tile_list(key, part):
    return support_lists(key)[0]


def draw_tile_counts(key, part):
    return support_lists(key)[1]


def embeddings(key):
    root_key = jax.random.fold_in(key, 11)
    sources = jax.random.normal(jax.random.fold_in(root_key, 1), (DIM, NSRC), jnp.float32)
    targets = jax.random.normal(jax.random.fold_in(root_key, 2), (DIM, NTGT), jnp.float32)
    return (jnp.clip(sources, -40.0, 40.0), jnp.clip(targets, -40.0, 40.0))


def draw_source_embed(key, part):
    return embeddings(key)[0]


def draw_target_embed(key, part):
    return embeddings(key)[1]


def block_scale(own_key, shape, shards, smallest, largest):
    level, own = 1.0, jax.random.fold_in(own_key, 6)
    for dim, parts in shards:
        draws = jnp.exp(jax.random.uniform(jax.random.fold_in(own, dim), (parts,), jnp.float32, smallest / len(shards), largest / len(shards)))
        level = level * jnp.repeat(draws, shape[dim] // parts).reshape([-1 if axis == dim else 1 for axis in range(len(shape))])
    return level


def setup_inputs(seed: int = 0) -> dict:
    key_of = jax.random.split(jax.random.key(seed), 7)
    source_embed = draw_source_embed(jax.random.fold_in(key_of[6], 71), 0)
    target_embed = draw_target_embed(jax.random.fold_in(key_of[6], 71), 0)
    source_mass = jnp.clip(jax.random.uniform(key_of[2], (NSRC,), jnp.float32, -2.0, 2.0) * block_scale(key_of[2], (NSRC,), ((0, 16),), -0.4, 0.0), -2.0, 2.0)
    target_mass = jnp.clip(jax.random.uniform(key_of[3], (NTGT,), jnp.float32, -2.0, 2.0) * block_scale(key_of[3], (NTGT,), ((0, 32),), -0.4, 0.0), -2.0, 2.0)
    tile_list = draw_tile_list(jax.random.fold_in(key_of[6], 71), 0)
    tile_counts = draw_tile_counts(jax.random.fold_in(key_of[6], 71), 0)
    return dict(source_embed=source_embed, target_embed=target_embed, source_mass=source_mass, target_mass=target_mass, tile_list=tile_list, tile_counts=tile_counts)


entropic = 0.1
lowest = -1e30


def pair_combine(earlier, later):
    highest = jnp.maximum(earlier[0], later[0])
    return highest, earlier[1] * jnp.exp(earlier[0] - highest) + later[1] * jnp.exp(later[0] - highest)


def block_terms(sources, source_norms, targets, target_norms, potential, row_block, col_block, to_rows):
    features = sources.shape[0]
    left_block = lax.dynamic_slice_in_dim(sources, row_block * TILE, TILE, 1)
    right_block = lax.dynamic_slice_in_dim(targets, col_block * TILE, TILE, 1)
    inner_products = lax.dot_general(left_block, right_block, (((0,), (0,)), ((), ())), precision=lax.Precision.HIGHEST, preferred_element_type=jnp.float32)
    left_norms = lax.dynamic_slice_in_dim(source_norms, row_block * TILE, TILE)
    right_norms = lax.dynamic_slice_in_dim(target_norms, col_block * TILE, TILE)
    cost_tile = (left_norms[:, None] + right_norms[None, :] - 2.0 * inner_products) / (2.0 * features)
    if to_rows:
        values = lax.dynamic_slice_in_dim(potential, col_block * TILE, TILE)
        scores = (values[None, :] - cost_tile) / entropic
        block_max = jnp.max(scores, axis=1)
        block_total = jnp.sum(jnp.exp(scores - block_max[:, None]), axis=1)
        return row_block * TILE, block_max, block_total
    values = lax.dynamic_slice_in_dim(potential, row_block * TILE, TILE)
    scores = (values[:, None] - cost_tile) / entropic
    block_max = jnp.max(scores, axis=0)
    block_total = jnp.sum(jnp.exp(scores - block_max[None, :]), axis=0)
    return col_block * TILE, block_max, block_total


def sweep_tiles(tile_list, tile_counts, sources, source_norms, targets, target_norms, potential, to_rows):
    slot_count = tile_list.shape[3]
    live_slots = (jnp.arange(slot_count, dtype=jnp.int32)[None, None, :] < tile_counts[:, :, None]).reshape(-1)
    row_blocks = jnp.maximum(tile_list[:, :, 0, :].reshape(-1), 0).astype(jnp.int32)
    col_blocks = jnp.maximum(tile_list[:, :, 1, :].reshape(-1), 0).astype(jnp.int32)
    length = sources.shape[1] if to_rows else targets.shape[1]
    start_carry = (jnp.full((length,), lowest, jnp.float32), jnp.zeros((length,), jnp.float32))

    def visit(running, visit_item):
        row_block, col_block, usable = visit_item
        offset, block_max, block_total = block_terms(sources, source_norms, targets, target_norms, potential, row_block, col_block, to_rows)
        previous = (lax.dynamic_slice_in_dim(running[0], offset, TILE), lax.dynamic_slice_in_dim(running[1], offset, TILE))
        merged = pair_combine(previous, (block_max, block_total))
        new_max = jnp.where(usable, merged[0], previous[0])
        new_total = jnp.where(usable, merged[1], previous[1])
        return (lax.dynamic_update_slice_in_dim(running[0], new_max, offset, 0), lax.dynamic_update_slice_in_dim(running[1], new_total, offset, 0)), None

    (maxima, totals), unused = lax.scan(visit, start_carry, (row_blocks, col_blocks, live_slots))
    return maxima + jnp.log(totals)


def reference(source_embed, target_embed, source_mass, target_mass, tile_list, tile_counts):
    source_norms = jnp.sum(source_embed * source_embed, axis=0)
    target_norms = jnp.sum(target_embed * target_embed, axis=0)
    source_side = jnp.zeros((source_embed.shape[1],), jnp.float32)
    target_side = jnp.zeros((target_embed.shape[1],), jnp.float32)
    for iteration in range(ITERS):
        source_side = entropic * (source_mass - sweep_tiles(tile_list, tile_counts, source_embed, source_norms, target_embed, target_norms, target_side, True))
        target_side = entropic * (target_mass - sweep_tiles(tile_list, tile_counts, source_embed, source_norms, target_embed, target_norms, source_side, False))
    return source_side, target_side
```

```python
import functools
import math

import jax
import jax.numpy as jnp
from jax import lax
from jax.experimental import pallas as pl
from jax.experimental.pallas import tpu as pltpu
from jax.sharding import PartitionSpec as P

TILE = 256
ITERS = 3
RING_Y = 8
CORES = 2
SPAN = 32

entropic = 0.1
dead_cost = 1e30
log2e = math.log2(math.e)
MESH = pl.DeviceIdType.MESH
LANES = 128


def ring_offsets(size):
    return sorted(range(1, size), key=lambda k: -min(k, size - k))


def wait_bytes(ref, sem):
    pltpu.make_async_copy(ref, ref, sem).wait()


def split_three(x):
    high = x.astype(jnp.bfloat16)
    rest = x - high.astype(jnp.float32)
    middle = rest.astype(jnp.bfloat16)
    low = (rest - middle.astype(jnp.float32)).astype(jnp.bfloat16)
    return high, middle, low


def combine(parts):
    highest = functools.reduce(jnp.maximum, parts)
    total = functools.reduce(jnp.add, [jnp.exp2(part - highest) for part in parts])
    return highest + jnp.log2(total)


def make_kernel(n_row, n_col, ring_y, cells, dim):
    ring_x = n_col // ring_y
    ring_z = n_row // CORES
    blocks = cells // LANES
    src_rows = dim // n_col
    tgt_rows = dim // n_row
    per = max(src_rows, tgt_rows)
    steps = dim // per
    tiles = cells // TILE
    x_offsets = ring_offsets(ring_x)
    y_offsets = ring_offsets(ring_y)
    z_offsets = [(0, 1)] + [(dz, dc) for dz in range(1, ring_z) for dc in range(CORES)]
    z_offsets.sort(key=lambda o: -min(o[0], ring_z - o[0]))

    def kernel(
        src_ref,
        tgt_ref,
        smass_ref,
        tmass_ref,
        list_ref,
        count_ref,
        out_ref,
        gsrc,
        gtgt,
        left,
        right,
        cost,
        cost_t,
        penalty,
        spread,
        part_x,
        part_y,
        part_z,
        got_x,
        got_y,
        got_z,
        gather_send,
        gather_recv,
        send_x,
        send_y,
        send_z,
        recv_x,
        recv_y,
        recv_z,
    ):
        row = lax.axis_index("row")
        col = lax.axis_index("col")
        x, y = col // ring_y, col % ring_y
        z, core = row // CORES, row % CORES
        x_peers = [(row, (x + dx) % ring_x * ring_y + y) for dx in x_offsets]
        y_peers = [(row, x * ring_y + (y + dy) % ring_y) for dy in y_offsets]
        z_peers = [((z + dz) % ring_z * CORES + (core + dc) % CORES, col) for dz, dc in z_offsets]

        barrier = pltpu.get_barrier_semaphore()
        for peer in y_peers + z_peers + x_peers:
            pl.semaphore_signal(barrier, inc=1, device_id=peer, device_id_type=MESH)

        own_src = gsrc.at[pl.ds(col * (blocks * src_rows), blocks * src_rows)]
        own_tgt = gtgt.at[pl.ds(row * (blocks * tgt_rows), blocks * tgt_rows)]
        for b in range(blocks):
            own_src[b * src_rows : (b + 1) * src_rows, :] = src_ref[:, b * LANES : (b + 1) * LANES]
            own_tgt[b * tgt_rows : (b + 1) * tgt_rows, :] = tgt_ref[:, b * LANES : (b + 1) * LANES]

        pl.semaphore_wait(barrier, len(x_peers) + len(y_peers) + len(z_peers))

        def send(src, dst, send_sem, recv_sem, peer):
            pltpu.make_async_remote_copy(
                src_ref=src,
                dst_ref=dst,
                send_sem=send_sem,
                recv_sem=recv_sem,
                device_id=peer,
                device_id_type=MESH,
            ).start()

        for peer in y_peers:
            send(own_src, own_src, gather_send.at[0], gather_recv.at[0], peer)
        for peer in z_peers:
            send(own_tgt, own_tgt, gather_send.at[1], gather_recv.at[1], peer)

        slots = list_ref[0, 0]
        slot_count = slots.shape[1]
        tile_ids = (slots[0:1, :] - row * tiles) * tiles + (slots[1:2, :] - col * tiles)
        live = lax.broadcasted_iota(jnp.int32, (1, slot_count), 1) < count_ref[...]
        tile_ids = jnp.where(live, tile_ids, -1)
        wanted = lax.broadcasted_iota(jnp.int32, (tiles * tiles * 8, slot_count), 0) // 8
        hits = jnp.where(wanted == tile_ids, 1.0, 0.0)
        found = jnp.max(hits, axis=1, keepdims=True)
        penalty[...] = jnp.broadcast_to(jnp.where(found > 0.5, 0.0, dead_cost), penalty.shape)

        unit = log2e / (entropic * 2.0 * dim)

        def load_features(ref, b, rows):
            found = []
            for q in range(per):
                start = q // rows * (blocks * rows) + b * rows + q % rows
                found.append(ref[pl.Slice(start, steps, per * blocks), :])
            return jnp.concatenate(found, axis=0)

        depth = left.shape[0]
        extra_rows = depth - 6 * dim

        def operands(gathered, out, rows, scale, is_left):
            for b in range(blocks):
                lanes = slice(b * LANES, (b + 1) * LANES)
                values = load_features(gathered, b, rows)
                norms = jnp.sum(values * values, axis=0, keepdims=True) * unit
                high, middle, low = split_three(values * scale if scale != 1.0 else values)
                order = (high, high, middle, middle, high, low)
                if not is_left:
                    order = (high, middle, high, middle, low, high)
                for k, term in enumerate(order):
                    out[k * dim : (k + 1) * dim, lanes] = term
                parts = [p.astype(jnp.float32) for p in split_three(norms)]
                one = jnp.ones((1, LANES), jnp.float32)
                pieces = parts + [one] * 3 if is_left else [one] * 3 + parts
                index = lax.broadcasted_iota(jnp.int32, (extra_rows, LANES), 0)
                extra = jnp.zeros((extra_rows, LANES), jnp.float32)
                for k, piece in enumerate(pieces):
                    extra = jnp.where(index == k, piece, extra)
                out[6 * dim :, lanes] = extra.astype(jnp.bfloat16)

        def fill(dst, lhs, rhs, major, minor):
            def one_row(rb, carry):
                rows = pl.ds(pl.multiple_of(rb * TILE, TILE), TILE)
                block = lhs[:, rows]
                for cb in range(tiles):
                    product = lax.dot_general(
                        block,
                        rhs[:, cb * TILE : (cb + 1) * TILE],
                        (((0,), (0,)), ((), ())),
                        preferred_element_type=jnp.float32,
                    )
                    tile = rb * major + cb * minor
                    extra = penalty[pl.ds(pl.multiple_of(tile * 8, 8), 8), :]
                    dst[rows, cb * TILE : (cb + 1) * TILE] = product + jnp.broadcast_to(
                        extra[0:1, 0:1], product.shape
                    )
                return carry

            lax.fori_loop(0, tiles, one_row, 0)

        def local_lse(costs, potential):
            turned = potential.T
            for b in range(blocks):
                spread[b * LANES : (b + 1) * LANES, :] = jnp.broadcast_to(
                    turned[:, b : b + 1], (LANES, LANES)
                )

            def fold(values, op):
                return op(values.reshape(SPAN // 8, 8, LANES), axis=0)

            def max_step(g, carry):
                rows = pl.ds(pl.multiple_of(g * SPAN, SPAN), SPAN)
                shift = spread[rows, :]
                return tuple(
                    jnp.maximum(
                        carry[b],
                        fold(shift - costs[rows, b * LANES : (b + 1) * LANES], jnp.max),
                    )
                    for b in range(blocks)
                )

            start = tuple(jnp.full((8, LANES), -3e38, jnp.float32) for b in range(blocks))
            maxima = lax.fori_loop(0, cells // SPAN, max_step, start)
            maxima = tuple(
                jnp.broadcast_to(jnp.max(m, axis=0, keepdims=True), (8, LANES)) for m in maxima
            )
            tall = tuple(jnp.broadcast_to(m[0:1], (SPAN, LANES)) for m in maxima)

            def sum_step(g, carry):
                rows = pl.ds(pl.multiple_of(g * SPAN, SPAN), SPAN)
                shift = spread[rows, :]
                return tuple(
                    carry[b]
                    + fold(
                        jnp.exp2((shift - costs[rows, b * LANES : (b + 1) * LANES]) - tall[b]),
                        jnp.sum,
                    )
                    for b in range(blocks)
                )

            start = tuple(jnp.zeros((8, LANES), jnp.float32) for b in range(blocks))
            totals = lax.fori_loop(0, cells // SPAN, sum_step, start)
            index = lax.broadcasted_iota(jnp.int32, (blocks, LANES), 0)
            highest = jnp.zeros((blocks, LANES), jnp.float32)
            total = jnp.ones((blocks, LANES), jnp.float32)
            for b in range(blocks):
                highest = jnp.where(index == b, maxima[b][0:1], highest)
                total = jnp.where(index == b, jnp.sum(totals[b], axis=0, keepdims=True), total)
            return highest + jnp.log2(total)

        wait_bytes(gsrc.at[pl.ds(0, len(y_peers) * blocks * src_rows)], gather_recv.at[0])
        group = ring_y * blocks * src_rows
        own_group = gsrc.at[pl.ds(x * group, group)]
        for peer in x_peers:
            send(own_group, own_group, gather_send.at[2], gather_recv.at[2], peer)
        wait_bytes(gtgt.at[pl.ds(0, len(z_peers) * blocks * tgt_rows)], gather_recv.at[1])
        operands(gtgt, right, tgt_rows, 1.0, False)
        wait_bytes(gsrc.at[pl.ds(0, len(x_peers) * group)], gather_recv.at[2])
        operands(gsrc, left, src_rows, -2.0 * unit, True)
        fill(cost_t, right, left, 1, tiles)

        source_mass = smass_ref[...] * log2e
        target_mass = tmass_ref[...] * log2e

        def iterate(turn, carry):
            target_side = carry[1]
            part_x[turn] = local_lse(cost_t, target_side)
            for k, peer in enumerate(x_peers):
                send(part_x.at[turn], got_x.at[turn, k], send_x, recv_x.at[turn], peer)

            @pl.when(turn == 0)
            def fill_cost():
                fill(cost, left, right, tiles, 1)

            wait_bytes(got_x.at[turn], recv_x.at[turn])
            part_y[turn] = combine([part_x[turn]] + [got_x[turn, k] for k in range(len(x_peers))])
            for k, peer in enumerate(y_peers):
                send(part_y.at[turn], got_y.at[turn, k], send_y, recv_y.at[turn], peer)
            wait_bytes(got_y.at[turn], recv_y.at[turn])
            lse = combine([part_y[turn]] + [got_y[turn, k] for k in range(len(y_peers))])
            source_side = source_mass - lse

            part_z[turn] = local_lse(cost, source_side)
            for k, peer in enumerate(z_peers):
                send(part_z.at[turn], got_z.at[turn, k], send_z, recv_z.at[turn], peer)
            wait_bytes(got_z.at[turn], recv_z.at[turn])
            lse = combine([part_z[turn]] + [got_z[turn, k] for k in range(len(z_peers))])
            return source_side, target_mass - lse

        zero = jnp.zeros((blocks, LANES), jnp.float32)
        source_side, target_side = lax.fori_loop(0, ITERS, iterate, (zero, zero))
        out_ref[0] = source_side
        out_ref[1] = target_side

        wait_bytes(gsrc.at[pl.ds(0, len(y_peers) * blocks * src_rows)], gather_send.at[0])
        wait_bytes(gtgt.at[pl.ds(0, len(z_peers) * blocks * tgt_rows)], gather_send.at[1])
        wait_bytes(gsrc.at[pl.ds(0, len(x_peers) * group)], gather_send.at[2])
        wait_bytes(got_x, send_x)
        wait_bytes(got_y, send_y)
        wait_bytes(got_z, send_z)

    def vector(count):
        return pltpu.VMEM((ITERS, count, blocks, LANES), jnp.float32)

    depth = 6 * dim + LANES
    scratch = [
        pltpu.VMEM((dim * blocks, LANES), jnp.float32),
        pltpu.VMEM((dim * blocks, LANES), jnp.float32),
        pltpu.VMEM((depth, cells), jnp.bfloat16),
        pltpu.VMEM((depth, cells), jnp.bfloat16),
        pltpu.VMEM((cells, cells), jnp.float32),
        pltpu.VMEM((cells, cells), jnp.float32),
        pltpu.VMEM((tiles * tiles * 8, LANES), jnp.float32),
        pltpu.VMEM((cells, LANES), jnp.float32),
        pltpu.VMEM((ITERS, blocks, LANES), jnp.float32),
        pltpu.VMEM((ITERS, blocks, LANES), jnp.float32),
        pltpu.VMEM((ITERS, blocks, LANES), jnp.float32),
        vector(len(x_offsets)),
        vector(len(y_offsets)),
        vector(len(z_offsets)),
        pltpu.SemaphoreType.DMA((3,)),
        pltpu.SemaphoreType.DMA((3,)),
        pltpu.SemaphoreType.DMA,
        pltpu.SemaphoreType.DMA,
        pltpu.SemaphoreType.DMA,
        pltpu.SemaphoreType.DMA((ITERS,)),
        pltpu.SemaphoreType.DMA((ITERS,)),
        pltpu.SemaphoreType.DMA((ITERS,)),
    ]
    return kernel, scratch


def shards(n_row, n_col, source_embed, target_embed, source_mass, target_mass, tile_list, tile_counts):
    cells = source_embed.shape[1]
    dim = source_embed.shape[0] * n_col
    blocks = cells // LANES
    kernel, scratch = make_kernel(n_row, n_col, RING_Y, cells, dim)
    whole = pl.BlockSpec(memory_space=pltpu.VMEM)
    sides = pl.pallas_call(
        kernel,
        out_shape=jax.ShapeDtypeStruct((2, blocks, LANES), jnp.float32),
        in_specs=[whole] * 6,
        out_specs=whole,
        scratch_shapes=scratch,
        compiler_params=pltpu.CompilerParams(collective_id=0, has_side_effects=True),
        name="sinkhorn",
    )(
        source_embed,
        target_embed,
        source_mass.reshape(blocks, LANES),
        target_mass.reshape(blocks, LANES),
        tile_list,
        tile_counts,
    )
    sides = sides * (entropic / log2e)
    return sides[0].reshape(cells), sides[1].reshape(cells)


def solution(mesh):
    in_specs = (
        P("col", "row"),
        P("row", "col"),
        P("row"),
        P("col"),
        P("row", "col", None, None),
        P("row", "col"),
    )
    out_specs = (P("row"), P("col"))
    body = functools.partial(shards, mesh.shape["row"], mesh.shape["col"])
    return jax.shard_map(body, mesh=mesh, in_specs=in_specs, out_specs=out_specs, check_vma=False)
```

```python
import functools
import math

import jax
import jax.numpy as jnp
from jax import lax
from jax.experimental import pallas as pl
from jax.experimental.pallas import tpu as pltpu
from jax.sharding import PartitionSpec as P

TILE = 256
ITERS = 3
RING_Y = 8
CORES = 2
SPAN = 64
UNROLL = 4

entropic = 0.1
dead_cost = 1e30
log2e = math.log2(math.e)
MESH = pl.DeviceIdType.MESH
LANES = 128


def blocks_of(cells):
    return cells // LANES


def ring_offsets(size):
    return sorted(range(1, size), key=lambda k: -min(k, size - k))


def wait_bytes(ref, sem):
    pltpu.make_async_copy(ref, ref, sem).wait()


def split_three(x):
    high = x.astype(jnp.bfloat16)
    rest = x - high.astype(jnp.float32)
    middle = rest.astype(jnp.bfloat16)
    low = (rest - middle.astype(jnp.float32)).astype(jnp.bfloat16)
    return high, middle, low


def combine(parts):
    highest = functools.reduce(jnp.maximum, parts)
    total = functools.reduce(jnp.add, [jnp.exp2(part - highest) for part in parts])
    return highest + jnp.log2(total)


def make_kernel(n_row, n_col, ring_y, cells, dim, slot_count):
    ring_x = n_col // ring_y
    ring_z = n_row // CORES
    blocks = blocks_of(cells)
    src_rows = dim // n_col
    tgt_rows = dim // n_row
    per = max(src_rows, tgt_rows)
    steps = dim // per
    src_size = src_rows * blocks_of(cells)
    tgt_size = tgt_rows * blocks_of(cells)
    tiles = cells // TILE
    x_offsets = ring_offsets(ring_x)
    y_offsets = ring_offsets(ring_y)
    z_offsets = [(0, 1)] + [(dz, dc) for dz in range(1, ring_z) for dc in range(CORES)]
    z_offsets.sort(key=lambda o: -min(o[0], ring_z - o[0]))
    chain_offsets = ring_offsets(ring_z)
    plane_offsets = [(dx, dy) for dx in range(ring_x) for dy in range(ring_y) if dx or dy]
    plane_offsets.sort(key=lambda o: -min(o[0], ring_x - o[0]) - min(o[1], ring_y - o[1]))

    def kernel(
        src_hbm,
        tgt_hbm,
        smass_hbm,
        tmass_hbm,
        list_hbm,
        count_hbm,
        source_out,
        target_out,
        src_ref,
        tgt_ref,
        smass_ref,
        tmass_ref,
        list_ref,
        count_ref,
        gsrc,
        gtgt,
        left,
        right,
        cost,
        cost_t,
        penalty,
        spread,
        part_row,
        part_col,
        got_row,
        got_col,
        load_sem,
        gather_send,
        y_recv,
        z_recv,
        x_recv,
        pair_recv,
        row_send,
        col_send,
        row_recv,
        col_recv,
    ):
        row = lax.axis_index("row")
        col = lax.axis_index("col")
        x, y = col // ring_y, col % ring_y
        z, core = row // CORES, row % CORES
        x_peers = [(row, (x + dx) % ring_x * ring_y + y) for dx in x_offsets]
        y_peers = [(row, x * ring_y + (y + dy) % ring_y) for dy in y_offsets]
        chain_peers = [((z + dz) % ring_z * CORES + core, col) for dz in chain_offsets]
        partner = (z * CORES + (core + 1) % CORES, col)
        z_peers = [((z + dz) % ring_z * CORES + (core + dc) % CORES, col) for dz, dc in z_offsets]
        plane_peers = [
            (row, (x + dx) % ring_x * ring_y + (y + dy) % ring_y) for dx, dy in plane_offsets
        ]

        loads = [
            pltpu.make_async_copy(hbm, ref, load_sem.at[k])
            for k, (hbm, ref) in enumerate(
                [
                    (src_hbm, src_ref),
                    (tgt_hbm, tgt_ref),
                    (smass_hbm, smass_ref),
                    (tmass_hbm, tmass_ref),
                    (list_hbm, list_ref),
                    (count_hbm, count_ref),
                ]
            )
        ]
        for load in loads:
            load.start()
        barrier = pltpu.get_barrier_semaphore()
        greeted = y_peers + z_peers + x_peers
        for peer in greeted:
            pl.semaphore_signal(barrier, inc=1, device_id=peer, device_id_type=MESH)

        def src_chunk(owner):
            return gsrc.at[pl.ds(pl.multiple_of(owner * src_size, src_size), src_size)]

        def tgt_chunk(owner):
            return gtgt.at[pl.ds(pl.multiple_of(owner * tgt_size, tgt_size), tgt_size)]

        own_src = src_chunk(col)
        own_tgt = tgt_chunk(row)
        for load in loads:
            load.wait()
        for b in range(blocks):
            own_src[b * src_rows : (b + 1) * src_rows, :] = src_ref[:, b * LANES : (b + 1) * LANES]
            own_tgt[b * tgt_rows : (b + 1) * tgt_rows, :] = tgt_ref[:, b * LANES : (b + 1) * LANES]

        pl.semaphore_wait(barrier, len(greeted))

        def send(src, dst, send_sem, recv_sem, peer):
            pltpu.make_async_remote_copy(
                src_ref=src,
                dst_ref=dst,
                send_sem=send_sem,
                recv_sem=recv_sem,
                device_id=peer,
                device_id_type=MESH,
            ).start()

        for k, peer in enumerate(y_peers):
            send(own_src, own_src, gather_send.at[0], y_recv.at[k], peer)
        for k, peer in enumerate(chain_peers):
            send(own_tgt, own_tgt, gather_send.at[1], z_recv.at[k], peer)
        for peer in x_peers:
            send(own_src, own_src, gather_send.at[2], x_recv, peer)
        send(own_tgt, own_tgt, gather_send.at[3], pair_recv, partner)

        slots = list_ref[0, 0]
        tile_ids = (slots[0:1, :] - row * tiles) * tiles + (slots[1:2, :] - col * tiles)
        live = lax.broadcasted_iota(jnp.int32, (1, slot_count), 1) < count_ref[...]
        tile_ids = jnp.where(live, tile_ids, -1)
        wanted = lax.broadcasted_iota(jnp.int32, (tiles * tiles * 8, slot_count), 0) // 8
        hits = jnp.where(wanted == tile_ids, 1.0, 0.0)
        found = jnp.max(hits, axis=1, keepdims=True)
        penalty[...] = jnp.broadcast_to(jnp.where(found > 0.5, 0.0, dead_cost), penalty.shape)

        unit = log2e / (entropic * 2.0 * dim)

        def load_features(ref, b, rows):
            found = []
            for q in range(per):
                start = q // rows * (blocks * rows) + b * rows + q % rows
                found.append(ref[pl.Slice(start, steps, per * blocks), :])
            return jnp.concatenate(found, axis=0)

        depth = left.shape[0]
        extra_rows = depth - 6 * dim

        def operands(gathered, out, rows, scale, is_left):
            for b in range(blocks):
                lanes = slice(b * LANES, (b + 1) * LANES)
                values = load_features(gathered, b, rows)
                norms = jnp.sum(values * values, axis=0, keepdims=True) * unit
                high, middle, low = split_three(values * scale if scale != 1.0 else values)
                order = (high, high, middle, middle, high, low)
                if not is_left:
                    order = (high, middle, high, middle, low, high)
                for k, term in enumerate(order):
                    out[k * dim : (k + 1) * dim, lanes] = term
                parts = [p.astype(jnp.float32) for p in split_three(norms)]
                one = jnp.ones((1, LANES), jnp.float32)
                pieces = parts + [one] * 3 if is_left else [one] * 3 + parts
                index = lax.broadcasted_iota(jnp.int32, (extra_rows, LANES), 0)
                extra = jnp.zeros((extra_rows, LANES), jnp.float32)
                for k, piece in enumerate(pieces):
                    extra = jnp.where(index == k, piece, extra)
                out[6 * dim :, lanes] = extra.astype(jnp.bfloat16)

        def fill(dst, lhs, rhs, major, minor):
            def one_row(rb, carry):
                rows = pl.ds(pl.multiple_of(rb * TILE, TILE), TILE)
                block = lhs[:, rows]
                for cb in range(tiles):
                    product = lax.dot_general(
                        block,
                        rhs[:, cb * TILE : (cb + 1) * TILE],
                        (((0,), (0,)), ((), ())),
                        preferred_element_type=jnp.float32,
                    )
                    tile = rb * major + cb * minor
                    extra = penalty[pl.ds(pl.multiple_of(tile * 8, 8), 8), :]
                    dst[rows, cb * TILE : (cb + 1) * TILE] = product + jnp.broadcast_to(
                        extra[0:1, 0:1], product.shape
                    )
                return carry

            lax.fori_loop(0, tiles, one_row, 0)

        def local_lse(costs, potential):
            turned = potential.T
            for b in range(blocks):
                spread[b * LANES : (b + 1) * LANES, :] = jnp.broadcast_to(
                    turned[:, b : b + 1], (LANES, LANES)
                )

            def step(g, carry):
                rows = pl.ds(pl.multiple_of(g * SPAN, SPAN), SPAN)
                shift = spread[rows, :]
                result = []
                for b in range(blocks):
                    highest, total = carry[b]
                    scores = shift - costs[rows, b * LANES : (b + 1) * LANES]
                    scores = scores.reshape(SPAN // 8, 8, LANES)
                    raised = jnp.maximum(highest, jnp.max(scores, axis=0))
                    fresh = jnp.sum(jnp.exp2(scores - raised[None]), axis=0)
                    result.append((raised, total * jnp.exp2(highest - raised) + fresh))
                return tuple(result)

            low = jnp.full((8, LANES), -3e38, jnp.float32)
            none = jnp.zeros((8, LANES), jnp.float32)
            pairs = lax.fori_loop(
                0, cells // SPAN, step, tuple((low, none) for b in range(blocks)), unroll=UNROLL
            )
            index = lax.broadcasted_iota(jnp.int32, (blocks, LANES), 0)
            lse_max = jnp.zeros((blocks, LANES), jnp.float32)
            lse_sum = jnp.ones((blocks, LANES), jnp.float32)
            for b in range(blocks):
                highest, total = pairs[b]
                top = jnp.max(highest, axis=0, keepdims=True)
                total = jnp.sum(total * jnp.exp2(highest - top), axis=0, keepdims=True)
                lse_max = jnp.where(index == b, top, lse_max)
                lse_sum = jnp.where(index == b, total, lse_sum)
            return lse_max + jnp.log2(lse_sum)

        y_order = sorted(range(len(y_offsets)), key=lambda k: -k)
        z_order = sorted(range(len(chain_offsets)), key=lambda k: -k)
        for i in range(max(len(y_order), len(z_order))):
            if i < len(y_order):
                k = y_order[i]
                chunk = src_chunk(x * ring_y + (y + ring_y - y_offsets[k]) % ring_y)
                wait_bytes(chunk, y_recv.at[k])
                for peer in x_peers:
                    send(chunk, chunk, gather_send.at[2], x_recv, peer)
            if i < len(z_order):
                k = z_order[i]
                chunk = tgt_chunk((z + ring_z - chain_offsets[k]) % ring_z * CORES + core)
                wait_bytes(chunk, z_recv.at[k])
                send(chunk, chunk, gather_send.at[3], pair_recv, partner)

        wait_bytes(gtgt.at[pl.ds(0, ring_z * tgt_size)], pair_recv)
        operands(gtgt, right, tgt_rows, 1.0, False)
        wait_bytes(gsrc.at[pl.ds(0, len(x_peers) * ring_y * src_size)], x_recv)
        operands(gsrc, left, src_rows, -2.0 * unit, True)
        fill(cost_t, right, left, 1, tiles)

        source_mass = smass_ref[...] * log2e
        target_mass = tmass_ref[...] * log2e

        def iterate(turn, carry):
            target_side = carry[1]
            part_row[turn] = local_lse(cost_t, target_side)
            for k, peer in enumerate(plane_peers):
                send(part_row.at[turn], got_row.at[turn, k], row_send, row_recv.at[turn], peer)

            @pl.when(turn == 0)
            def fill_cost():
                fill(cost, left, right, tiles, 1)

            wait_bytes(got_row.at[turn], row_recv.at[turn])
            lse = combine([part_row[turn]] + [got_row[turn, k] for k in range(len(plane_peers))])
            source_side = source_mass - lse

            part_col[turn] = local_lse(cost, source_side)
            for k, peer in enumerate(z_peers):
                send(part_col.at[turn], got_col.at[turn, k], col_send, col_recv.at[turn], peer)
            wait_bytes(got_col.at[turn], col_recv.at[turn])
            lse = combine([part_col[turn]] + [got_col[turn, k] for k in range(len(z_peers))])
            return source_side, target_mass - lse

        zero = jnp.zeros((blocks, LANES), jnp.float32)
        source_side, target_side = lax.fori_loop(0, ITERS, iterate, (zero, zero))
        source_out[...] = source_side
        target_out[...] = target_side

        wait_bytes(gsrc.at[pl.ds(0, len(y_peers) * src_size)], gather_send.at[0])
        wait_bytes(gtgt.at[pl.ds(0, len(chain_peers) * tgt_size)], gather_send.at[1])
        wait_bytes(gsrc.at[pl.ds(0, len(x_peers) * ring_y * src_size)], gather_send.at[2])
        wait_bytes(gtgt.at[pl.ds(0, ring_z * tgt_size)], gather_send.at[3])
        wait_bytes(got_row, row_send)
        wait_bytes(got_col, col_send)

    def vector(count):
        return pltpu.VMEM((ITERS, count, blocks, LANES), jnp.float32)

    depth = 6 * dim + LANES
    scratch = [
        pltpu.VMEM((src_rows, cells), jnp.float32),
        pltpu.VMEM((tgt_rows, cells), jnp.float32),
        pltpu.VMEM((blocks, LANES), jnp.float32),
        pltpu.VMEM((blocks, LANES), jnp.float32),
        pltpu.VMEM((1, 1, 2, slot_count), jnp.int32),
        pltpu.VMEM((1, 1), jnp.int32),
        pltpu.VMEM((dim * blocks, LANES), jnp.float32),
        pltpu.VMEM((dim * blocks, LANES), jnp.float32),
        pltpu.VMEM((depth, cells), jnp.bfloat16),
        pltpu.VMEM((depth, cells), jnp.bfloat16),
        pltpu.VMEM((cells, cells), jnp.float32),
        pltpu.VMEM((cells, cells), jnp.float32),
        pltpu.VMEM((tiles * tiles * 8, LANES), jnp.float32),
        pltpu.VMEM((cells, LANES), jnp.float32),
        pltpu.VMEM((ITERS, blocks, LANES), jnp.float32),
        pltpu.VMEM((ITERS, blocks, LANES), jnp.float32),
        vector(len(plane_offsets)),
        vector(len(z_offsets)),
        pltpu.SemaphoreType.DMA((6,)),
        pltpu.SemaphoreType.DMA((4,)),
        pltpu.SemaphoreType.DMA((len(y_offsets),)),
        pltpu.SemaphoreType.DMA((len(chain_offsets),)),
        pltpu.SemaphoreType.DMA,
        pltpu.SemaphoreType.DMA,
        pltpu.SemaphoreType.DMA,
        pltpu.SemaphoreType.DMA,
        pltpu.SemaphoreType.DMA((ITERS,)),
        pltpu.SemaphoreType.DMA((ITERS,)),
    ]
    return kernel, scratch


def shards(n_row, n_col, source_embed, target_embed, source_mass, target_mass, tile_list, tile_counts):
    cells = source_embed.shape[1]
    dim = source_embed.shape[0] * n_col
    blocks = cells // LANES
    kernel, scratch = make_kernel(n_row, n_col, RING_Y, cells, dim, tile_list.shape[3])
    side = jax.ShapeDtypeStruct((blocks, LANES), jnp.float32)
    source_side, target_side = pl.pallas_call(
        kernel,
        out_shape=(side, side),
        in_specs=[pl.BlockSpec(memory_space=pl.ANY)] * 6,
        out_specs=[pl.BlockSpec(memory_space=pltpu.VMEM)] * 2,
        scratch_shapes=scratch,
        compiler_params=pltpu.CompilerParams(collective_id=0, has_side_effects=True),
        name="sinkhorn",
    )(
        source_embed,
        target_embed,
        source_mass.reshape(blocks, LANES),
        target_mass.reshape(blocks, LANES),
        tile_list,
        tile_counts,
    )
    unit = entropic / log2e
    return (source_side * unit).reshape(cells), (target_side * unit).reshape(cells)


def solution(mesh):
    in_specs = (
        P("col", "row"),
        P("row", "col"),
        P("row"),
        P("col"),
        P("row", "col", None, None),
        P("row", "col"),
    )
    out_specs = (P("row"), P("col"))
    body = functools.partial(shards, mesh.shape["row"], mesh.shape["col"])
    return jax.shard_map(body, mesh=mesh, in_specs=in_specs, out_specs=out_specs, check_vma=False)
```

```python
import functools
import math

import jax
import jax.numpy as jnp
from jax import lax
from jax.experimental import pallas as pl
from jax.experimental.pallas import tpu as pltpu
from jax.sharding import PartitionSpec as P

TILE = 256
ITERS = 3
RING_Y = 8
CORES = 2
SPAN = 64
UNROLL = 4
HALVES = 2

entropic = 0.1
dead_cost = 1e30
log2e = math.log2(math.e)
MESH = pl.DeviceIdType.MESH
LANES = 128


def ring_offsets(size):
    return sorted(range(1, size), key=lambda k: -min(k, size - k))


def wait_bytes(ref, sem):
    pltpu.make_async_copy(ref, ref, sem).wait()


def split_three(x):
    high = x.astype(jnp.bfloat16)
    rest = x - high.astype(jnp.float32)
    middle = rest.astype(jnp.bfloat16)
    low = (rest - middle.astype(jnp.float32)).astype(jnp.bfloat16)
    return high, middle, low


def combine(parts):
    highest = functools.reduce(jnp.maximum, parts)
    total = functools.reduce(jnp.add, [jnp.exp2(part - highest) for part in parts])
    return highest + jnp.log2(total)


def make_kernel(n_row, n_col, ring_y, cells, dim, slot_count):
    ring_x = n_col // ring_y
    ring_z = n_row // CORES
    blocks = cells // LANES
    src_rows = dim // n_col
    tgt_rows = dim // n_row
    per = max(src_rows, tgt_rows)
    steps = dim // per
    part = blocks // HALVES
    src_size = src_rows * blocks
    tgt_size = tgt_rows * blocks
    tiles = cells // TILE
    x_offsets = ring_offsets(ring_x)
    y_offsets = ring_offsets(ring_y)
    z_offsets = [(0, 1)] + [(dz, dc) for dz in range(1, ring_z) for dc in range(CORES)]
    z_offsets.sort(key=lambda o: -min(o[0], ring_z - o[0]))
    chain_offsets = ring_offsets(ring_z)
    plane_offsets = [(dx, dy) for dx in range(ring_x) for dy in range(ring_y) if dx or dy]
    plane_offsets.sort(key=lambda o: -min(o[0], ring_x - o[0]) - min(o[1], ring_y - o[1]))

    def kernel(
        src_hbm,
        tgt_hbm,
        smass_hbm,
        tmass_hbm,
        list_hbm,
        count_hbm,
        source_out,
        target_out,
        src_ref,
        tgt_ref,
        smass_ref,
        tmass_ref,
        list_ref,
        count_ref,
        gsrc,
        gtgt,
        left,
        right,
        cost,
        cost_t,
        penalty,
        spread,
        state,
        part_row,
        part_col,
        got_row,
        got_col,
        load_sem,
        gather_send,
        y_recv,
        z_recv,
        x_recv,
        pair_recv,
        row_send,
        col_send,
        row_recv,
        col_recv,
    ):
        row = lax.axis_index("row")
        col = lax.axis_index("col")
        x, y = col // ring_y, col % ring_y
        z, core = row // CORES, row % CORES
        x_peers = [(row, (x + dx) % ring_x * ring_y + y) for dx in x_offsets]
        y_peers = [(row, x * ring_y + (y + dy) % ring_y) for dy in y_offsets]
        chain_peers = [((z + dz) % ring_z * CORES + core, col) for dz in chain_offsets]
        partner = (z * CORES + (core + 1) % CORES, col)
        z_peers = [((z + dz) % ring_z * CORES + (core + dc) % CORES, col) for dz, dc in z_offsets]
        plane_peers = [
            (row, (x + dx) % ring_x * ring_y + (y + dy) % ring_y) for dx, dy in plane_offsets
        ]

        loads = [
            pltpu.make_async_copy(hbm, ref, load_sem.at[k])
            for k, (hbm, ref) in enumerate(
                [
                    (src_hbm, src_ref),
                    (tgt_hbm, tgt_ref),
                    (smass_hbm, smass_ref),
                    (tmass_hbm, tmass_ref),
                    (list_hbm, list_ref),
                    (count_hbm, count_ref),
                ]
            )
        ]
        for load in loads:
            load.start()
        barrier = pltpu.get_barrier_semaphore()
        greeted = y_peers + z_peers + x_peers
        for peer in greeted:
            pl.semaphore_signal(barrier, inc=1, device_id=peer, device_id_type=MESH)

        def src_chunk(owner):
            return gsrc.at[pl.ds(pl.multiple_of(owner * src_size, src_size), src_size)]

        def tgt_chunk(owner):
            return gtgt.at[pl.ds(pl.multiple_of(owner * tgt_size, tgt_size), tgt_size)]

        own_src = src_chunk(col)
        own_tgt = tgt_chunk(row)
        for load in loads:
            load.wait()
        for b in range(blocks):
            own_src[b * src_rows : (b + 1) * src_rows, :] = src_ref[:, b * LANES : (b + 1) * LANES]
            own_tgt[b * tgt_rows : (b + 1) * tgt_rows, :] = tgt_ref[:, b * LANES : (b + 1) * LANES]

        pl.semaphore_wait(barrier, len(greeted))

        def send(src, dst, send_sem, recv_sem, peer):
            pltpu.make_async_remote_copy(
                src_ref=src,
                dst_ref=dst,
                send_sem=send_sem,
                recv_sem=recv_sem,
                device_id=peer,
                device_id_type=MESH,
            ).start()

        for k, peer in enumerate(y_peers):
            send(own_src, own_src, gather_send.at[0], y_recv.at[k], peer)
        for k, peer in enumerate(chain_peers):
            send(own_tgt, own_tgt, gather_send.at[1], z_recv.at[k], peer)
        for peer in x_peers:
            send(own_src, own_src, gather_send.at[2], x_recv, peer)
        send(own_tgt, own_tgt, gather_send.at[3], pair_recv, partner)

        slots = list_ref[0, 0]
        tile_ids = (slots[0:1, :] - row * tiles) * tiles + (slots[1:2, :] - col * tiles)
        live = lax.broadcasted_iota(jnp.int32, (1, slot_count), 1) < count_ref[...]
        tile_ids = jnp.where(live, tile_ids, -1)
        wanted = lax.broadcasted_iota(jnp.int32, (tiles * tiles * 8, slot_count), 0) // 8
        hits = jnp.where(wanted == tile_ids, 1.0, 0.0)
        found = jnp.max(hits, axis=1, keepdims=True)
        penalty[...] = jnp.broadcast_to(jnp.where(found > 0.5, 0.0, dead_cost), penalty.shape)

        unit = log2e / (entropic * 2.0 * dim)

        def load_features(ref, b, rows):
            found = []
            for q in range(per):
                start = q // rows * (blocks * rows) + b * rows + q % rows
                found.append(ref[pl.Slice(start, steps, per * blocks), :])
            return jnp.concatenate(found, axis=0)

        depth = left.shape[0]
        extra_rows = depth - 6 * dim

        def operands(gathered, out, rows, scale, is_left):
            for b in range(blocks):
                lanes = slice(b * LANES, (b + 1) * LANES)
                values = load_features(gathered, b, rows)
                norms = jnp.sum(values * values, axis=0, keepdims=True) * unit
                high, middle, low = split_three(values * scale if scale != 1.0 else values)
                order = (high, high, middle, middle, high, low)
                if not is_left:
                    order = (high, middle, high, middle, low, high)
                for k, term in enumerate(order):
                    out[k * dim : (k + 1) * dim, lanes] = term
                parts = [p.astype(jnp.float32) for p in split_three(norms)]
                one = jnp.ones((1, LANES), jnp.float32)
                pieces = parts + [one] * 3 if is_left else [one] * 3 + parts
                index = lax.broadcasted_iota(jnp.int32, (extra_rows, LANES), 0)
                extra = jnp.zeros((extra_rows, LANES), jnp.float32)
                for k, piece in enumerate(pieces):
                    extra = jnp.where(index == k, piece, extra)
                out[6 * dim :, lanes] = extra.astype(jnp.bfloat16)

        def fill(dst, lhs, rhs, major, minor):
            def one_row(rb, carry):
                rows = pl.ds(pl.multiple_of(rb * TILE, TILE), TILE)
                block = lhs[:, rows]
                for cb in range(tiles):
                    product = lax.dot_general(
                        block,
                        rhs[:, cb * TILE : (cb + 1) * TILE],
                        (((0,), (0,)), ((), ())),
                        preferred_element_type=jnp.float32,
                    )
                    tile = rb * major + cb * minor
                    extra = penalty[pl.ds(pl.multiple_of(tile * 8, 8), 8), :]
                    dst[rows, cb * TILE : (cb + 1) * TILE] = product + jnp.broadcast_to(
                        extra[0:1, 0:1], product.shape
                    )
                return carry

            lax.fori_loop(0, tiles, one_row, 0)

        def spread_half(potential, half):
            turned = potential.T
            for b in range(part):
                start = (half * part + b) * LANES
                spread[start : start + LANES, :] = jnp.broadcast_to(
                    turned[:, b : b + 1], (LANES, LANES)
                )

        def sweep(costs, half, chosen, pairs):
            reach = cells // HALVES

            def step(g, carry):
                rows = pl.ds(pl.multiple_of(half * reach + g * SPAN, SPAN), SPAN)
                shift = spread[rows, :]
                result = []
                for b, (highest, total) in zip(chosen, carry):
                    scores = shift - costs[rows, b * LANES : (b + 1) * LANES]
                    scores = scores.reshape(SPAN // 8, 8, LANES)
                    raised = jnp.maximum(highest, jnp.max(scores, axis=0))
                    fresh = jnp.sum(jnp.exp2(scores - raised[None]), axis=0)
                    result.append((raised, total * jnp.exp2(highest - raised) + fresh))
                return tuple(result)

            return lax.fori_loop(0, reach // SPAN, step, tuple(pairs), unroll=UNROLL)

        def finish(pairs):
            index = lax.broadcasted_iota(jnp.int32, (part, LANES), 0)
            lse_max = jnp.zeros((part, LANES), jnp.float32)
            lse_sum = jnp.ones((part, LANES), jnp.float32)
            for b, (highest, total) in enumerate(pairs):
                top = jnp.max(highest, axis=0, keepdims=True)
                total = jnp.sum(total * jnp.exp2(highest - top), axis=0, keepdims=True)
                lse_max = jnp.where(index == b, top, lse_max)
                lse_sum = jnp.where(index == b, total, lse_sum)
            return lse_max + jnp.log2(lse_sum)

        def open_pass(costs, potential):
            spread_half(potential, 0)
            low = jnp.full((8, LANES), -3e38, jnp.float32)
            none = jnp.zeros((8, LANES), jnp.float32)
            pairs = sweep(costs, 0, range(blocks), [(low, none)] * blocks)
            for b, (highest, total) in enumerate(pairs):
                state[0, b] = highest
                state[1, b] = total

        def close_pass(costs, potential, emit):
            spread_half(potential, 1)
            for half in range(HALVES):
                chosen = range(half * part, (half + 1) * part)
                pairs = sweep(costs, 1, chosen, [(state[0, b], state[1, b]) for b in chosen])
                emit(half, finish(pairs))

        def merged(own, got, turn, half, count):
            return combine([own[turn, half]] + [got[turn, half, k] for k in range(count)])

        y_order = sorted(range(len(y_offsets)), key=lambda k: -k)
        z_order = sorted(range(len(chain_offsets)), key=lambda k: -k)
        for i in range(max(len(y_order), len(z_order))):
            if i < len(y_order):
                k = y_order[i]
                chunk = src_chunk(x * ring_y + (y + ring_y - y_offsets[k]) % ring_y)
                wait_bytes(chunk, y_recv.at[k])
                for peer in x_peers:
                    send(chunk, chunk, gather_send.at[2], x_recv, peer)
            if i < len(z_order):
                k = z_order[i]
                chunk = tgt_chunk((z + ring_z - chain_offsets[k]) % ring_z * CORES + core)
                wait_bytes(chunk, z_recv.at[k])
                send(chunk, chunk, gather_send.at[3], pair_recv, partner)

        wait_bytes(gtgt.at[pl.ds(0, ring_z * tgt_size)], pair_recv)
        operands(gtgt, right, tgt_rows, 1.0, False)
        wait_bytes(gsrc.at[pl.ds(0, len(x_peers) * ring_y * src_size)], x_recv)
        operands(gsrc, left, src_rows, -2.0 * unit, True)
        fill(cost_t, right, left, 1, tiles)

        source_mass = [smass_ref[h * part : (h + 1) * part, :] * log2e for h in range(HALVES)]
        target_mass = [tmass_ref[h * part : (h + 1) * part, :] * log2e for h in range(HALVES)]
        zero = jnp.zeros((part, LANES), jnp.float32)
        open_pass(cost_t, zero)

        def iterate(turn, target_late):
            def emit_row(half, lse):
                part_row[turn, half] = lse
                for k, peer in enumerate(plane_peers):
                    send(
                        part_row.at[turn, half],
                        got_row.at[turn, half, k],
                        row_send,
                        row_recv.at[turn, half],
                        peer,
                    )

            def emit_col(half, lse):
                part_col[turn, half] = lse
                for k, peer in enumerate(z_peers):
                    send(
                        part_col.at[turn, half],
                        got_col.at[turn, half, k],
                        col_send,
                        col_recv.at[turn, half],
                        peer,
                    )

            def source_half(half):
                wait_bytes(got_row.at[turn, half], row_recv.at[turn, half])
                lse = merged(part_row, got_row, turn, half, len(plane_peers))
                source_out[half * part : (half + 1) * part, :] = source_mass[half] - lse
                return source_mass[half] - lse

            def target_half(half):
                wait_bytes(got_col.at[turn, half], col_recv.at[turn, half])
                lse = merged(part_col, got_col, turn, half, len(z_peers))
                target_out[half * part : (half + 1) * part, :] = target_mass[half] - lse
                return target_mass[half] - lse

            close_pass(cost_t, target_late, emit_row)

            @pl.when(turn == 0)
            def fill_cost():
                fill(cost, left, right, tiles, 1)

            open_pass(cost, source_half(0))
            close_pass(cost, source_half(1), emit_col)
            target_early = target_half(0)

            @pl.when(turn < ITERS - 1)
            def next_pass():
                open_pass(cost_t, target_early)

            return target_half(1)

        lax.fori_loop(0, ITERS, iterate, zero)

        wait_bytes(gsrc.at[pl.ds(0, len(y_peers) * src_size)], gather_send.at[0])
        wait_bytes(gtgt.at[pl.ds(0, len(chain_peers) * tgt_size)], gather_send.at[1])
        wait_bytes(gsrc.at[pl.ds(0, len(x_peers) * ring_y * src_size)], gather_send.at[2])
        wait_bytes(gtgt.at[pl.ds(0, ring_z * tgt_size)], gather_send.at[3])
        wait_bytes(got_row, row_send)
        wait_bytes(got_col, col_send)

    def vector(count):
        return pltpu.VMEM((ITERS, HALVES, count, part, LANES), jnp.float32)

    depth = 6 * dim + LANES
    scratch = [
        pltpu.VMEM((src_rows, cells), jnp.float32),
        pltpu.VMEM((tgt_rows, cells), jnp.float32),
        pltpu.VMEM((blocks, LANES), jnp.float32),
        pltpu.VMEM((blocks, LANES), jnp.float32),
        pltpu.VMEM((1, 1, 2, slot_count), jnp.int32),
        pltpu.VMEM((1, 1), jnp.int32),
        pltpu.VMEM((dim * blocks, LANES), jnp.float32),
        pltpu.VMEM((dim * blocks, LANES), jnp.float32),
        pltpu.VMEM((depth, cells), jnp.bfloat16),
        pltpu.VMEM((depth, cells), jnp.bfloat16),
        pltpu.VMEM((cells, cells), jnp.float32),
        pltpu.VMEM((cells, cells), jnp.float32),
        pltpu.VMEM((tiles * tiles * 8, LANES), jnp.float32),
        pltpu.VMEM((cells, LANES), jnp.float32),
        pltpu.VMEM((2, blocks, 8, LANES), jnp.float32),
        pltpu.VMEM((ITERS, HALVES, part, LANES), jnp.float32),
        pltpu.VMEM((ITERS, HALVES, part, LANES), jnp.float32),
        vector(len(plane_offsets)),
        vector(len(z_offsets)),
        pltpu.SemaphoreType.DMA((6,)),
        pltpu.SemaphoreType.DMA((4,)),
        pltpu.SemaphoreType.DMA((len(y_offsets),)),
        pltpu.SemaphoreType.DMA((len(chain_offsets),)),
        pltpu.SemaphoreType.DMA,
        pltpu.SemaphoreType.DMA,
        pltpu.SemaphoreType.DMA,
        pltpu.SemaphoreType.DMA,
        pltpu.SemaphoreType.DMA((ITERS, HALVES)),
        pltpu.SemaphoreType.DMA((ITERS, HALVES)),
    ]
    return kernel, scratch


def shards(n_row, n_col, source_embed, target_embed, source_mass, target_mass, tile_list, tile_counts):
    cells = source_embed.shape[1]
    dim = source_embed.shape[0] * n_col
    blocks = cells // LANES
    kernel, scratch = make_kernel(n_row, n_col, RING_Y, cells, dim, tile_list.shape[3])
    side = pltpu.VMEM((blocks, LANES), jnp.float32)
    source_side, target_side = pl.pallas_call(
        kernel,
        out_shape=(side, side),
        in_specs=[pl.BlockSpec(memory_space=pl.ANY)] * 6,
        out_specs=[pl.BlockSpec(memory_space=pltpu.VMEM)] * 2,
        scratch_shapes=scratch,
        compiler_params=pltpu.CompilerParams(collective_id=0, has_side_effects=True),
        name="sinkhorn",
    )(
        source_embed,
        target_embed,
        source_mass.reshape(blocks, LANES),
        target_mass.reshape(blocks, LANES),
        tile_list,
        tile_counts,
    )
    unit = entropic / log2e
    return (source_side * unit).reshape(cells), (target_side * unit).reshape(cells)


def solution(mesh):
    in_specs = (
        P("col", "row"),
        P("row", "col"),
        P("row"),
        P("col"),
        P("row", "col", None, None),
        P("row", "col"),
    )
    out_specs = (P("row"), P("col"))
    body = functools.partial(shards, mesh.shape["row"], mesh.shape["col"])
    return jax.shard_map(body, mesh=mesh, in_specs=in_specs, out_specs=out_specs, check_vma=False)
```

```python
import functools
import math

import jax
import jax.numpy as jnp
from jax import lax
from jax.experimental import pallas as pl
from jax.experimental.pallas import tpu as pltpu
from jax.sharding import PartitionSpec as P

TILE = 256
ITERS = 3
RING_Y = 8
CORES = 2
SPAN = 64
UNROLL = 4
HALVES = 2

entropic = 0.1
dead_cost = 1e30
log2e = math.log2(math.e)
MESH = pl.DeviceIdType.MESH
LANES = 128


def ring_offsets(size):
    return sorted(range(1, size), key=lambda k: -min(k, size - k))


def wait_bytes(ref, sem):
    pltpu.make_async_copy(ref, ref, sem).wait()


def split_three(x):
    high = x.astype(jnp.bfloat16)
    rest = x - high.astype(jnp.float32)
    middle = rest.astype(jnp.bfloat16)
    low = (rest - middle.astype(jnp.float32)).astype(jnp.bfloat16)
    return high, middle, low


def combine(parts):
    highest = functools.reduce(jnp.maximum, parts)
    total = functools.reduce(jnp.add, [jnp.exp2(part - highest) for part in parts])
    return highest + jnp.log2(total)


def make_kernel(n_row, n_col, ring_y, cells, dim, slot_count):
    ring_x = n_col // ring_y
    ring_z = n_row // CORES
    blocks = cells // LANES
    src_rows = dim // n_col
    tgt_rows = dim // n_row
    per = max(src_rows, tgt_rows)
    steps = dim // per
    part = blocks // HALVES
    src_size = src_rows * blocks
    tgt_size = tgt_rows * blocks
    tiles = cells // TILE
    x_offsets = ring_offsets(ring_x)
    y_offsets = ring_offsets(ring_y)
    z_offsets = [(0, 1)] + [(dz, dc) for dz in range(1, ring_z) for dc in range(CORES)]
    z_offsets.sort(key=lambda o: -min(o[0], ring_z - o[0]))
    chain_offsets = ring_offsets(ring_z)
    def reach_of(dx, dy):
        return min(dx, ring_x - dx) + min(dy, ring_y - dy)

    plane_offsets = [(dx, dy) for dx in range(ring_x) for dy in range(ring_y) if dx or dy]
    plane_offsets.sort(key=lambda o: -reach_of(*o))
    plane_far = sum(2 * reach_of(*o) > ring_x // 2 + ring_y // 2 for o in plane_offsets)
    plane_near = len(plane_offsets) - plane_far
    z_far = sum(2 * min(dz, ring_z - dz) > ring_z // 2 for dz, dc in z_offsets)
    z_near = len(z_offsets) - z_far

    def kernel(
        src_hbm,
        tgt_hbm,
        smass_hbm,
        tmass_hbm,
        list_hbm,
        count_hbm,
        source_out,
        target_out,
        src_ref,
        tgt_ref,
        smass_ref,
        tmass_ref,
        list_ref,
        count_ref,
        gsrc,
        gtgt,
        left,
        right,
        cost,
        cost_t,
        penalty,
        spread,
        state,
        part_row,
        part_col,
        far_row,
        far_col,
        near_row,
        near_col,
        load_sem,
        gather_send,
        y_recv,
        z_recv,
        x_recv,
        pair_recv,
        row_send,
        col_send,
        far_row_recv,
        far_col_recv,
        near_row_recv,
        near_col_recv,
    ):
        row = lax.axis_index("row")
        col = lax.axis_index("col")
        x, y = col // ring_y, col % ring_y
        z, core = row // CORES, row % CORES
        x_peers = [(row, (x + dx) % ring_x * ring_y + y) for dx in x_offsets]
        y_peers = [(row, x * ring_y + (y + dy) % ring_y) for dy in y_offsets]
        chain_peers = [((z + dz) % ring_z * CORES + core, col) for dz in chain_offsets]
        partner = (z * CORES + (core + 1) % CORES, col)
        z_peers = [((z + dz) % ring_z * CORES + (core + dc) % CORES, col) for dz, dc in z_offsets]
        plane_peers = [
            (row, (x + dx) % ring_x * ring_y + (y + dy) % ring_y) for dx, dy in plane_offsets
        ]

        loads = [
            pltpu.make_async_copy(hbm, ref, load_sem.at[k])
            for k, (hbm, ref) in enumerate(
                [
                    (src_hbm, src_ref),
                    (tgt_hbm, tgt_ref),
                    (smass_hbm, smass_ref),
                    (tmass_hbm, tmass_ref),
                    (list_hbm, list_ref),
                    (count_hbm, count_ref),
                ]
            )
        ]
        for load in loads:
            load.start()
        barrier = pltpu.get_barrier_semaphore()
        greeted = y_peers + z_peers + x_peers
        for peer in greeted:
            pl.semaphore_signal(barrier, inc=1, device_id=peer, device_id_type=MESH)

        def src_chunk(owner):
            return gsrc.at[pl.ds(pl.multiple_of(owner * src_size, src_size), src_size)]

        def tgt_chunk(owner):
            return gtgt.at[pl.ds(pl.multiple_of(owner * tgt_size, tgt_size), tgt_size)]

        own_src = src_chunk(col)
        own_tgt = tgt_chunk(row)
        for load in loads:
            load.wait()
        for b in range(blocks):
            own_src[b * src_rows : (b + 1) * src_rows, :] = src_ref[:, b * LANES : (b + 1) * LANES]
            own_tgt[b * tgt_rows : (b + 1) * tgt_rows, :] = tgt_ref[:, b * LANES : (b + 1) * LANES]

        pl.semaphore_wait(barrier, len(greeted))

        def send(src, dst, send_sem, recv_sem, peer):
            pltpu.make_async_remote_copy(
                src_ref=src,
                dst_ref=dst,
                send_sem=send_sem,
                recv_sem=recv_sem,
                device_id=peer,
                device_id_type=MESH,
            ).start()

        for k, peer in enumerate(y_peers):
            send(own_src, own_src, gather_send.at[0], y_recv.at[k], peer)
        for k, peer in enumerate(chain_peers):
            send(own_tgt, own_tgt, gather_send.at[1], z_recv.at[k], peer)
        for peer in x_peers:
            send(own_src, own_src, gather_send.at[2], x_recv, peer)
        send(own_tgt, own_tgt, gather_send.at[3], pair_recv, partner)

        slots = list_ref[0, 0]
        tile_ids = (slots[0:1, :] - row * tiles) * tiles + (slots[1:2, :] - col * tiles)
        live = lax.broadcasted_iota(jnp.int32, (1, slot_count), 1) < count_ref[...]
        tile_ids = jnp.where(live, tile_ids, -1)
        wanted = lax.broadcasted_iota(jnp.int32, (tiles * tiles * 8, slot_count), 0) // 8
        hits = jnp.where(wanted == tile_ids, 1.0, 0.0)
        found = jnp.max(hits, axis=1, keepdims=True)
        penalty[...] = jnp.broadcast_to(jnp.where(found > 0.5, 0.0, dead_cost), penalty.shape)

        unit = log2e / (entropic * 2.0 * dim)

        def load_features(ref, b, rows):
            found = []
            for q in range(per):
                start = q // rows * (blocks * rows) + b * rows + q % rows
                found.append(ref[pl.Slice(start, steps, per * blocks), :])
            return jnp.concatenate(found, axis=0)

        depth = left.shape[0]
        extra_rows = depth - 6 * dim

        def operands(gathered, out, rows, scale, is_left):
            for b in range(blocks):
                lanes = slice(b * LANES, (b + 1) * LANES)
                values = load_features(gathered, b, rows)
                norms = jnp.sum(values * values, axis=0, keepdims=True) * unit
                high, middle, low = split_three(values * scale if scale != 1.0 else values)
                order = (high, high, middle, middle, high, low)
                if not is_left:
                    order = (high, middle, high, middle, low, high)
                for k, term in enumerate(order):
                    out[k * dim : (k + 1) * dim, lanes] = term
                parts = [p.astype(jnp.float32) for p in split_three(norms)]
                one = jnp.ones((1, LANES), jnp.float32)
                pieces = parts + [one] * 3 if is_left else [one] * 3 + parts
                index = lax.broadcasted_iota(jnp.int32, (extra_rows, LANES), 0)
                extra = jnp.zeros((extra_rows, LANES), jnp.float32)
                for k, piece in enumerate(pieces):
                    extra = jnp.where(index == k, piece, extra)
                out[6 * dim :, lanes] = extra.astype(jnp.bfloat16)

        def fill(dst, lhs, rhs, major, minor):
            def one_row(rb, carry):
                rows = pl.ds(pl.multiple_of(rb * TILE, TILE), TILE)
                block = lhs[:, rows]
                for cb in range(tiles):
                    product = lax.dot_general(
                        block,
                        rhs[:, cb * TILE : (cb + 1) * TILE],
                        (((0,), (0,)), ((), ())),
                        preferred_element_type=jnp.float32,
                    )
                    tile = rb * major + cb * minor
                    extra = penalty[pl.ds(pl.multiple_of(tile * 8, 8), 8), :]
                    dst[rows, cb * TILE : (cb + 1) * TILE] = product + jnp.broadcast_to(
                        extra[0:1, 0:1], product.shape
                    )
                return carry

            lax.fori_loop(0, tiles, one_row, 0)

        def spread_half(potential, half):
            turned = potential.T
            for b in range(part):
                start = (half * part + b) * LANES
                spread[start : start + LANES, :] = jnp.broadcast_to(
                    turned[:, b : b + 1], (LANES, LANES)
                )

        def sweep(costs, half, chosen, pairs):
            reach = cells // HALVES

            def step(g, carry):
                rows = pl.ds(pl.multiple_of(half * reach + g * SPAN, SPAN), SPAN)
                shift = spread[rows, :]
                result = []
                for b, (highest, total) in zip(chosen, carry):
                    scores = shift - costs[rows, b * LANES : (b + 1) * LANES]
                    scores = scores.reshape(SPAN // 8, 8, LANES)
                    raised = jnp.maximum(highest, jnp.max(scores, axis=0))
                    fresh = jnp.sum(jnp.exp2(scores - raised[None]), axis=0)
                    result.append((raised, total * jnp.exp2(highest - raised) + fresh))
                return tuple(result)

            return lax.fori_loop(0, reach // SPAN, step, tuple(pairs), unroll=UNROLL)

        def finish(pairs):
            index = lax.broadcasted_iota(jnp.int32, (part, LANES), 0)
            lse_max = jnp.zeros((part, LANES), jnp.float32)
            lse_sum = jnp.ones((part, LANES), jnp.float32)
            for b, (highest, total) in enumerate(pairs):
                top = jnp.max(highest, axis=0, keepdims=True)
                total = jnp.sum(total * jnp.exp2(highest - top), axis=0, keepdims=True)
                lse_max = jnp.where(index == b, top, lse_max)
                lse_sum = jnp.where(index == b, total, lse_sum)
            return lse_max + jnp.log2(lse_sum)

        def open_pass(costs, potential):
            spread_half(potential, 0)
            low = jnp.full((8, LANES), -3e38, jnp.float32)
            none = jnp.zeros((8, LANES), jnp.float32)
            pairs = sweep(costs, 0, range(blocks), [(low, none)] * blocks)
            for b, (highest, total) in enumerate(pairs):
                state[0, b] = highest
                state[1, b] = total

        def close_pass(costs, potential, emit):
            spread_half(potential, 1)
            for half in range(HALVES):
                chosen = range(half * part, (half + 1) * part)
                pairs = sweep(costs, 1, chosen, [(state[0, b], state[1, b]) for b in chosen])
                emit(half, finish(pairs))

        def merged(own, far, near, turn, half):
            parts = [far[turn, half, k] for k in range(far.shape[2])]
            parts += [near[turn, k, half] for k in range(near.shape[1])]
            return combine([own[turn, half]] + parts)

        def emit_to(peers, own, far, near, sends, far_recv, near_recv, turn, half, lse):
            own[turn, half] = lse
            far_count = far.shape[2]
            for k, peer in enumerate(peers[:far_count]):
                send(
                    own.at[turn, half],
                    far.at[turn, half, k],
                    sends.at[0],
                    far_recv.at[turn, half],
                    peer,
                )
            if half == HALVES - 1:
                for k, peer in enumerate(peers[far_count:]):
                    send(own.at[turn], near.at[turn, k], sends.at[1], near_recv.at[turn], peer)

        arrivals = [(min(d, ring_y - d), 0, k) for k, d in enumerate(y_offsets)]
        arrivals += [(min(d, ring_z - d) + 1.5, 1, k) for k, d in enumerate(chain_offsets)]
        for when, chain, k in sorted(arrivals):
            if chain:
                chunk = tgt_chunk((z + ring_z - chain_offsets[k]) % ring_z * CORES + core)
                wait_bytes(chunk, z_recv.at[k])
                send(chunk, chunk, gather_send.at[3], pair_recv, partner)
            else:
                chunk = src_chunk(x * ring_y + (y + ring_y - y_offsets[k]) % ring_y)
                wait_bytes(chunk, y_recv.at[k])
                for peer in x_peers:
                    send(chunk, chunk, gather_send.at[2], x_recv, peer)

        wait_bytes(gtgt.at[pl.ds(0, ring_z * tgt_size)], pair_recv)
        operands(gtgt, right, tgt_rows, 1.0, False)
        wait_bytes(gsrc.at[pl.ds(0, len(x_peers) * ring_y * src_size)], x_recv)
        operands(gsrc, left, src_rows, -2.0 * unit, True)
        fill(cost_t, right, left, 1, tiles)

        source_mass = [smass_ref[h * part : (h + 1) * part, :] * log2e for h in range(HALVES)]
        target_mass = [tmass_ref[h * part : (h + 1) * part, :] * log2e for h in range(HALVES)]
        zero = jnp.zeros((part, LANES), jnp.float32)
        open_pass(cost_t, zero)

        def iterate(turn, target_late):
            emit_row = functools.partial(
                emit_to,
                plane_peers,
                part_row,
                far_row,
                near_row,
                row_send,
                far_row_recv,
                near_row_recv,
                turn,
            )
            emit_col = functools.partial(
                emit_to,
                z_peers,
                part_col,
                far_col,
                near_col,
                col_send,
                far_col_recv,
                near_col_recv,
                turn,
            )

            def source_half(half):
                wait_bytes(far_row.at[turn, half], far_row_recv.at[turn, half])
                if half == 0:
                    wait_bytes(near_row.at[turn], near_row_recv.at[turn])
                lse = merged(part_row, far_row, near_row, turn, half)
                source_out[half * part : (half + 1) * part, :] = source_mass[half] - lse
                return source_mass[half] - lse

            def target_half(half):
                wait_bytes(far_col.at[turn, half], far_col_recv.at[turn, half])
                if half == 0:
                    wait_bytes(near_col.at[turn], near_col_recv.at[turn])
                lse = merged(part_col, far_col, near_col, turn, half)
                target_out[half * part : (half + 1) * part, :] = target_mass[half] - lse
                return target_mass[half] - lse

            close_pass(cost_t, target_late, emit_row)

            @pl.when(turn == 0)
            def fill_cost():
                fill(cost, left, right, tiles, 1)

            open_pass(cost, source_half(0))
            close_pass(cost, source_half(1), emit_col)
            target_early = target_half(0)

            @pl.when(turn < ITERS - 1)
            def next_pass():
                open_pass(cost_t, target_early)

            return target_half(1)

        lax.fori_loop(0, ITERS, iterate, zero)

        wait_bytes(gsrc.at[pl.ds(0, len(y_peers) * src_size)], gather_send.at[0])
        wait_bytes(gtgt.at[pl.ds(0, len(chain_peers) * tgt_size)], gather_send.at[1])
        wait_bytes(gsrc.at[pl.ds(0, len(x_peers) * ring_y * src_size)], gather_send.at[2])
        wait_bytes(gtgt.at[pl.ds(0, ring_z * tgt_size)], gather_send.at[3])
        wait_bytes(far_row, row_send.at[0])
        wait_bytes(near_row, row_send.at[1])
        wait_bytes(far_col, col_send.at[0])
        wait_bytes(near_col, col_send.at[1])

    def far_slots(count):
        return pltpu.VMEM((ITERS, HALVES, count, part, LANES), jnp.float32)

    def near_slots(count):
        return pltpu.VMEM((ITERS, count, HALVES, part, LANES), jnp.float32)

    depth = 6 * dim + LANES
    scratch = [
        pltpu.VMEM((src_rows, cells), jnp.float32),
        pltpu.VMEM((tgt_rows, cells), jnp.float32),
        pltpu.VMEM((blocks, LANES), jnp.float32),
        pltpu.VMEM((blocks, LANES), jnp.float32),
        pltpu.VMEM((1, 1, 2, slot_count), jnp.int32),
        pltpu.VMEM((1, 1), jnp.int32),
        pltpu.VMEM((dim * blocks, LANES), jnp.float32),
        pltpu.VMEM((dim * blocks, LANES), jnp.float32),
        pltpu.VMEM((depth, cells), jnp.bfloat16),
        pltpu.VMEM((depth, cells), jnp.bfloat16),
        pltpu.VMEM((cells, cells), jnp.float32),
        pltpu.VMEM((cells, cells), jnp.float32),
        pltpu.VMEM((tiles * tiles * 8, LANES), jnp.float32),
        pltpu.VMEM((cells, LANES), jnp.float32),
        pltpu.VMEM((2, blocks, 8, LANES), jnp.float32),
        pltpu.VMEM((ITERS, HALVES, part, LANES), jnp.float32),
        pltpu.VMEM((ITERS, HALVES, part, LANES), jnp.float32),
        far_slots(plane_far),
        far_slots(z_far),
        near_slots(plane_near),
        near_slots(z_near),
        pltpu.SemaphoreType.DMA((6,)),
        pltpu.SemaphoreType.DMA((4,)),
        pltpu.SemaphoreType.DMA((len(y_offsets),)),
        pltpu.SemaphoreType.DMA((len(chain_offsets),)),
        pltpu.SemaphoreType.DMA,
        pltpu.SemaphoreType.DMA,
        pltpu.SemaphoreType.DMA((2,)),
        pltpu.SemaphoreType.DMA((2,)),
        pltpu.SemaphoreType.DMA((ITERS, HALVES)),
        pltpu.SemaphoreType.DMA((ITERS, HALVES)),
        pltpu.SemaphoreType.DMA((ITERS,)),
        pltpu.SemaphoreType.DMA((ITERS,)),
    ]
    return kernel, scratch


def shards(n_row, n_col, source_embed, target_embed, source_mass, target_mass, tile_list, tile_counts):
    cells = source_embed.shape[1]
    dim = source_embed.shape[0] * n_col
    blocks = cells // LANES
    kernel, scratch = make_kernel(n_row, n_col, RING_Y, cells, dim, tile_list.shape[3])
    side = pltpu.VMEM((blocks, LANES), jnp.float32)
    source_side, target_side = pl.pallas_call(
        kernel,
        out_shape=(side, side),
        in_specs=[pl.BlockSpec(memory_space=pl.ANY)] * 6,
        out_specs=[pl.BlockSpec(memory_space=pltpu.VMEM)] * 2,
        scratch_shapes=scratch,
        compiler_params=pltpu.CompilerParams(collective_id=0, has_side_effects=True),
        name="sinkhorn",
    )(
        source_embed,
        target_embed,
        source_mass.reshape(blocks, LANES),
        target_mass.reshape(blocks, LANES),
        tile_list,
        tile_counts,
    )
    unit = entropic / log2e
    return (source_side * unit).reshape(cells), (target_side * unit).reshape(cells)


def solution(mesh):
    in_specs = (
        P("col", "row"),
        P("row", "col"),
        P("row"),
        P("col"),
        P("row", "col", None, None),
        P("row", "col"),
    )
    out_specs = (P("row"), P("col"))
    body = functools.partial(shards, mesh.shape["row"], mesh.shape["col"])
    return jax.shard_map(body, mesh=mesh, in_specs=in_specs, out_specs=out_specs, check_vma=False)
```

```python
import functools
import math

import jax
import jax.numpy as jnp
from jax import lax
from jax.experimental import pallas as pl
from jax.experimental.pallas import tpu as pltpu
from jax.sharding import PartitionSpec as P

TILE = 256
ITERS = 3
RING_Y = 8
CORES = 2
SPAN = 64
UNROLL = 4
HALVES = 2

entropic = 0.1
dead_cost = 1e30
log2e = math.log2(math.e)
MESH = pl.DeviceIdType.MESH
LANES = 128


def wait_bytes(ref, sem):
    pltpu.make_async_copy(ref, ref, sem).wait()


def split_three(x):
    high = x.astype(jnp.bfloat16)
    rest = x - high.astype(jnp.float32)
    middle = rest.astype(jnp.bfloat16)
    low = (rest - middle.astype(jnp.float32)).astype(jnp.bfloat16)
    return high, middle, low


def combine(parts):
    highest = functools.reduce(jnp.maximum, parts)
    total = functools.reduce(jnp.add, [jnp.exp2(part - highest) for part in parts])
    return highest + jnp.log2(total)


def make_kernel(n_row, n_col, ring_y, cells, dim, slot_count):
    ring_x = n_col // ring_y
    ring_z = n_row // CORES
    blocks = cells // LANES
    src_rows = dim // n_col
    tgt_rows = dim // n_row
    per = max(src_rows, tgt_rows)
    steps = dim // per
    part = blocks // HALVES
    src_size = src_rows * blocks
    tgt_size = tgt_rows * blocks
    tiles = cells // TILE
    rest_chunks = (ring_x - 1) * ring_y - (ring_y if ring_x > 3 else 0)
    z_offsets = [(0, 1)] + [(dz, dc) for dz in range(1, ring_z) for dc in range(CORES)]
    z_offsets.sort(key=lambda o: -min(o[0], ring_z - o[0]))
    def reach_of(dx, dy):
        return min(dx, ring_x - dx) + min(dy, ring_y - dy)

    plane_offsets = [(dx, dy) for dx in range(ring_x) for dy in range(ring_y) if dx or dy]
    plane_offsets.sort(key=lambda o: -reach_of(*o))
    plane_far = sum(2 * reach_of(*o) > ring_x // 2 + ring_y // 2 for o in plane_offsets)
    plane_near = len(plane_offsets) - plane_far
    z_far = sum(2 * min(dz, ring_z - dz) > ring_z // 2 for dz, dc in z_offsets)
    z_near = len(z_offsets) - z_far

    def kernel(
        src_hbm,
        tgt_hbm,
        smass_hbm,
        tmass_hbm,
        list_hbm,
        count_hbm,
        source_out,
        target_out,
        src_ref,
        tgt_ref,
        smass_ref,
        tmass_ref,
        list_ref,
        count_ref,
        gsrc,
        gtgt,
        left,
        right,
        cost,
        cost_t,
        penalty,
        spread,
        state,
        part_row,
        part_col,
        far_row,
        far_col,
        near_row,
        near_col,
        load_sem,
        gather_send,
        y_recv,
        z_recv,
        x_recv,
        x_relay,
        pair_recv,
        row_send,
        col_send,
        far_row_recv,
        far_col_recv,
        near_row_recv,
        near_col_recv,
    ):
        row = lax.axis_index("row")
        col = lax.axis_index("col")
        x, y = col // ring_y, col % ring_y
        z, core = row // CORES, row % CORES
        def x_step(dx):
            return (row, (x + dx + ring_x) % ring_x * ring_y + y)

        def y_step(dy):
            return (row, x * ring_y + (y + dy + ring_y) % ring_y)

        def z_step(dz):
            return ((z + dz + ring_z) % ring_z * CORES + core, col)

        def beside(step, size):
            return [step(1), step(-1)] if size > 2 else [step(1)] if size > 1 else []

        partner = (z * CORES + (core + 1) % CORES, col)
        z_peers = [((z + dz) % ring_z * CORES + (core + dc) % CORES, col) for dz, dc in z_offsets]
        plane_peers = [
            (row, (x + dx) % ring_x * ring_y + (y + dy) % ring_y) for dx, dy in plane_offsets
        ]

        loads = [
            pltpu.make_async_copy(hbm, ref, load_sem.at[k])
            for k, (hbm, ref) in enumerate(
                [
                    (src_hbm, src_ref),
                    (tgt_hbm, tgt_ref),
                    (smass_hbm, smass_ref),
                    (tmass_hbm, tmass_ref),
                    (list_hbm, list_ref),
                    (count_hbm, count_ref),
                ]
            )
        ]
        for load in loads:
            load.start()
        barrier = pltpu.get_barrier_semaphore()
        greeted = [partner] + beside(y_step, ring_y) + beside(z_step, ring_z) + beside(x_step, ring_x)
        for peer in greeted:
            pl.semaphore_signal(barrier, inc=1, device_id=peer, device_id_type=MESH)

        def src_chunk(owner):
            return gsrc.at[pl.ds(pl.multiple_of(owner * src_size, src_size), src_size)]

        def tgt_chunk(owner):
            return gtgt.at[pl.ds(pl.multiple_of(owner * tgt_size, tgt_size), tgt_size)]

        own_src = src_chunk(col)
        own_tgt = tgt_chunk(row)
        for load in loads:
            load.wait()
        for b in range(blocks):
            own_src[b * src_rows : (b + 1) * src_rows, :] = src_ref[:, b * LANES : (b + 1) * LANES]
            own_tgt[b * tgt_rows : (b + 1) * tgt_rows, :] = tgt_ref[:, b * LANES : (b + 1) * LANES]

        pl.semaphore_wait(barrier, len(greeted))

        def send(src, dst, send_sem, recv_sem, peer):
            pltpu.make_async_remote_copy(
                src_ref=src,
                dst_ref=dst,
                send_sem=send_sem,
                recv_sem=recv_sem,
                device_id=peer,
                device_id_type=MESH,
            ).start()

        def pass_on(chunk, step, size, distance, send_sem, recv):
            for way in (1, -1) if distance == 0 else (1 if distance > 0 else -1,):
                after = abs(distance) + 1
                limit = size // 2 if way > 0 else (size - 1) // 2
                if after <= limit:
                    slot = after - 1 if way > 0 else size // 2 + after - 1
                    send(chunk, chunk, send_sem, recv.at[slot], step(way))

        def hand_out(chunk, q):
            for way in (1, -1)[: min(ring_x - 1, 2)]:
                relayed = ring_x > 3 and (way > 0) == (q % 2 == 0)
                recv = x_relay.at[q] if relayed else x_recv
                send(chunk, chunk, gather_send.at[2], recv, x_step(way))

        pass_on(own_src, y_step, ring_y, 0, gather_send.at[0], y_recv)
        pass_on(own_tgt, z_step, ring_z, 0, gather_send.at[1], z_recv)
        hand_out(own_src, 0)
        send(own_tgt, own_tgt, gather_send.at[3], pair_recv, partner)

        slots = list_ref[0, 0]
        tile_ids = (slots[0:1, :] - row * tiles) * tiles + (slots[1:2, :] - col * tiles)
        live = lax.broadcasted_iota(jnp.int32, (1, slot_count), 1) < count_ref[...]
        tile_ids = jnp.where(live, tile_ids, -1)
        wanted = lax.broadcasted_iota(jnp.int32, (tiles * tiles * 8, slot_count), 0) // 8
        hits = jnp.where(wanted == tile_ids, 1.0, 0.0)
        found = jnp.max(hits, axis=1, keepdims=True)
        penalty[...] = jnp.broadcast_to(jnp.where(found > 0.5, 0.0, dead_cost), penalty.shape)

        unit = log2e / (entropic * 2.0 * dim)

        def load_features(ref, b, rows):
            found = []
            for q in range(per):
                start = q // rows * (blocks * rows) + b * rows + q % rows
                found.append(ref[pl.Slice(start, steps, per * blocks), :])
            return jnp.concatenate(found, axis=0)

        depth = left.shape[0]
        extra_rows = depth - 6 * dim

        def operands(gathered, out, rows, scale, is_left):
            for b in range(blocks):
                lanes = slice(b * LANES, (b + 1) * LANES)
                values = load_features(gathered, b, rows)
                norms = jnp.sum(values * values, axis=0, keepdims=True) * unit
                high, middle, low = split_three(values * scale if scale != 1.0 else values)
                order = (high, high, middle, middle, high, low)
                if not is_left:
                    order = (high, middle, high, middle, low, high)
                for k, term in enumerate(order):
                    out[k * dim : (k + 1) * dim, lanes] = term
                parts = [p.astype(jnp.float32) for p in split_three(norms)]
                one = jnp.ones((1, LANES), jnp.float32)
                pieces = parts + [one] * 3 if is_left else [one] * 3 + parts
                index = lax.broadcasted_iota(jnp.int32, (extra_rows, LANES), 0)
                extra = jnp.zeros((extra_rows, LANES), jnp.float32)
                for k, piece in enumerate(pieces):
                    extra = jnp.where(index == k, piece, extra)
                out[6 * dim :, lanes] = extra.astype(jnp.bfloat16)

        def fill(dst, lhs, rhs, major, minor):
            def one_row(rb, carry):
                rows = pl.ds(pl.multiple_of(rb * TILE, TILE), TILE)
                block = lhs[:, rows]
                for cb in range(tiles):
                    product = lax.dot_general(
                        block,
                        rhs[:, cb * TILE : (cb + 1) * TILE],
                        (((0,), (0,)), ((), ())),
                        preferred_element_type=jnp.float32,
                    )
                    tile = rb * major + cb * minor
                    extra = penalty[pl.ds(pl.multiple_of(tile * 8, 8), 8), :]
                    dst[rows, cb * TILE : (cb + 1) * TILE] = product + jnp.broadcast_to(
                        extra[0:1, 0:1], product.shape
                    )
                return carry

            lax.fori_loop(0, tiles, one_row, 0)

        def spread_half(potential, half):
            turned = potential.T
            for b in range(part):
                start = (half * part + b) * LANES
                spread[start : start + LANES, :] = jnp.broadcast_to(
                    turned[:, b : b + 1], (LANES, LANES)
                )

        def sweep(costs, half, chosen, pairs):
            reach = cells // HALVES

            def step(g, carry):
                rows = pl.ds(pl.multiple_of(half * reach + g * SPAN, SPAN), SPAN)
                shift = spread[rows, :]
                result = []
                for b, (highest, total) in zip(chosen, carry):
                    scores = shift - costs[rows, b * LANES : (b + 1) * LANES]
                    scores = scores.reshape(SPAN // 8, 8, LANES)
                    raised = jnp.maximum(highest, jnp.max(scores, axis=0))
                    fresh = jnp.sum(jnp.exp2(scores - raised[None]), axis=0)
                    result.append((raised, total * jnp.exp2(highest - raised) + fresh))
                return tuple(result)

            return lax.fori_loop(0, reach // SPAN, step, tuple(pairs), unroll=UNROLL)

        def finish(pairs):
            index = lax.broadcasted_iota(jnp.int32, (part, LANES), 0)
            lse_max = jnp.zeros((part, LANES), jnp.float32)
            lse_sum = jnp.ones((part, LANES), jnp.float32)
            for b, (highest, total) in enumerate(pairs):
                top = jnp.max(highest, axis=0, keepdims=True)
                total = jnp.sum(total * jnp.exp2(highest - top), axis=0, keepdims=True)
                lse_max = jnp.where(index == b, top, lse_max)
                lse_sum = jnp.where(index == b, total, lse_sum)
            return lse_max + jnp.log2(lse_sum)

        def open_pass(costs, potential):
            spread_half(potential, 0)
            low = jnp.full((8, LANES), -3e38, jnp.float32)
            none = jnp.zeros((8, LANES), jnp.float32)
            pairs = sweep(costs, 0, range(blocks), [(low, none)] * blocks)
            for b, (highest, total) in enumerate(pairs):
                state[0, b] = highest
                state[1, b] = total

        def close_pass(costs, potential, emit):
            spread_half(potential, 1)
            for half in range(HALVES):
                chosen = range(half * part, (half + 1) * part)
                pairs = sweep(costs, 1, chosen, [(state[0, b], state[1, b]) for b in chosen])
                emit(half, finish(pairs))

        def merged(own, far, near, turn, half):
            parts = [far[turn, half, k] for k in range(far.shape[2])]
            parts += [near[turn, k, half] for k in range(near.shape[1])]
            return combine([own[turn, half]] + parts)

        def emit_to(peers, own, far, near, sends, far_recv, near_recv, turn, half, lse):
            own[turn, half] = lse
            far_count = far.shape[2]
            for k, peer in enumerate(peers[:far_count]):
                send(
                    own.at[turn, half],
                    far.at[turn, half, k],
                    sends.at[0],
                    far_recv.at[turn, half],
                    peer,
                )
            if half == HALVES - 1:
                for k, peer in enumerate(peers[far_count:]):
                    send(own.at[turn], near.at[turn, k], sends.at[1], near_recv.at[turn], peer)

        events = []
        for size, kind in ((ring_y, 0), (ring_z, 1)):
            for d in range(1, size // 2 + 1):
                events.append((1.7 * d + 0.2 * kind, kind, d, d - 1))
            for d in range(1, (size - 1) // 2 + 1):
                events.append((1.7 * d + 0.2 * kind, kind, -d, size // 2 + d - 1))
        for q in range(ring_y if ring_x > 3 else 0):
            events.append((1.7 * min(q, ring_y - q) + 1.8, 2, q, q))
        for when, kind, d, slot in sorted(events):
            if kind == 0:
                chunk = src_chunk(x * ring_y + (y + ring_y - d) % ring_y)
                wait_bytes(chunk, y_recv.at[slot])
                pass_on(chunk, y_step, ring_y, d, gather_send.at[0], y_recv)
                hand_out(chunk, (ring_y - d) % ring_y)
            elif kind == 1:
                chunk = tgt_chunk((z + ring_z - d) % ring_z * CORES + core)
                wait_bytes(chunk, z_recv.at[slot])
                pass_on(chunk, z_step, ring_z, d, gather_send.at[1], z_recv)
                send(chunk, chunk, gather_send.at[3], pair_recv, partner)
            else:
                way = 1 if d % 2 == 0 else -1
                owner_x = (x + ring_x - way) % ring_x
                chunk = src_chunk(owner_x * ring_y + (y + d) % ring_y)
                wait_bytes(chunk, x_relay.at[slot])
                send(chunk, chunk, gather_send.at[2], x_recv, x_step(way))

        wait_bytes(gtgt.at[pl.ds(0, ring_z * tgt_size)], pair_recv)
        operands(gtgt, right, tgt_rows, 1.0, False)
        wait_bytes(gsrc.at[pl.ds(0, rest_chunks * src_size)], x_recv)
        operands(gsrc, left, src_rows, -2.0 * unit, True)
        fill(cost_t, right, left, 1, tiles)

        source_mass = [smass_ref[h * part : (h + 1) * part, :] * log2e for h in range(HALVES)]
        target_mass = [tmass_ref[h * part : (h + 1) * part, :] * log2e for h in range(HALVES)]
        zero = jnp.zeros((part, LANES), jnp.float32)
        open_pass(cost_t, zero)

        def iterate(turn, target_late):
            emit_row = functools.partial(
                emit_to,
                plane_peers,
                part_row,
                far_row,
                near_row,
                row_send,
                far_row_recv,
                near_row_recv,
                turn,
            )
            emit_col = functools.partial(
                emit_to,
                z_peers,
                part_col,
                far_col,
                near_col,
                col_send,
                far_col_recv,
                near_col_recv,
                turn,
            )

            def source_half(half):
                wait_bytes(far_row.at[turn, half], far_row_recv.at[turn, half])
                if half == 0:
                    wait_bytes(near_row.at[turn], near_row_recv.at[turn])
                lse = merged(part_row, far_row, near_row, turn, half)
                source_out[half * part : (half + 1) * part, :] = source_mass[half] - lse
                return source_mass[half] - lse

            def target_half(half):
                wait_bytes(far_col.at[turn, half], far_col_recv.at[turn, half])
                if half == 0:
                    wait_bytes(near_col.at[turn], near_col_recv.at[turn])
                lse = merged(part_col, far_col, near_col, turn, half)
                target_out[half * part : (half + 1) * part, :] = target_mass[half] - lse
                return target_mass[half] - lse

            close_pass(cost_t, target_late, emit_row)

            @pl.when(turn == 0)
            def fill_cost():
                fill(cost, left, right, tiles, 1)

            open_pass(cost, source_half(0))
            close_pass(cost, source_half(1), emit_col)
            target_early = target_half(0)

            @pl.when(turn < ITERS - 1)
            def next_pass():
                open_pass(cost_t, target_early)

            return target_half(1)

        lax.fori_loop(0, ITERS, iterate, zero)

        wait_bytes(gsrc.at[pl.ds(0, (ring_y - 1) * src_size)], gather_send.at[0])
        if ring_z > 1:
            wait_bytes(gtgt.at[pl.ds(0, (ring_z - 1) * tgt_size)], gather_send.at[1])
        wait_bytes(gsrc.at[pl.ds(0, (ring_x - 1) * ring_y * src_size)], gather_send.at[2])
        wait_bytes(gtgt.at[pl.ds(0, ring_z * tgt_size)], gather_send.at[3])
        wait_bytes(far_row, row_send.at[0])
        wait_bytes(near_row, row_send.at[1])
        wait_bytes(far_col, col_send.at[0])
        wait_bytes(near_col, col_send.at[1])

    def far_slots(count):
        return pltpu.VMEM((ITERS, HALVES, count, part, LANES), jnp.float32)

    def near_slots(count):
        return pltpu.VMEM((ITERS, count, HALVES, part, LANES), jnp.float32)

    depth = 6 * dim + LANES
    scratch = [
        pltpu.VMEM((src_rows, cells), jnp.float32),
        pltpu.VMEM((tgt_rows, cells), jnp.float32),
        pltpu.VMEM((blocks, LANES), jnp.float32),
        pltpu.VMEM((blocks, LANES), jnp.float32),
        pltpu.VMEM((1, 1, 2, slot_count), jnp.int32),
        pltpu.VMEM((1, 1), jnp.int32),
        pltpu.VMEM((dim * blocks, LANES), jnp.float32),
        pltpu.VMEM((dim * blocks, LANES), jnp.float32),
        pltpu.VMEM((depth, cells), jnp.bfloat16),
        pltpu.VMEM((depth, cells), jnp.bfloat16),
        pltpu.VMEM((cells, cells), jnp.float32),
        pltpu.VMEM((cells, cells), jnp.float32),
        pltpu.VMEM((tiles * tiles * 8, LANES), jnp.float32),
        pltpu.VMEM((cells, LANES), jnp.float32),
        pltpu.VMEM((2, blocks, 8, LANES), jnp.float32),
        pltpu.VMEM((ITERS, HALVES, part, LANES), jnp.float32),
        pltpu.VMEM((ITERS, HALVES, part, LANES), jnp.float32),
        far_slots(plane_far),
        far_slots(z_far),
        near_slots(plane_near),
        near_slots(z_near),
        pltpu.SemaphoreType.DMA((6,)),
        pltpu.SemaphoreType.DMA((4,)),
        pltpu.SemaphoreType.DMA((ring_y,)),
        pltpu.SemaphoreType.DMA((ring_z,)),
        pltpu.SemaphoreType.DMA,
        pltpu.SemaphoreType.DMA((ring_y,)),
        pltpu.SemaphoreType.DMA,
        pltpu.SemaphoreType.DMA((2,)),
        pltpu.SemaphoreType.DMA((2,)),
        pltpu.SemaphoreType.DMA((ITERS, HALVES)),
        pltpu.SemaphoreType.DMA((ITERS, HALVES)),
        pltpu.SemaphoreType.DMA((ITERS,)),
        pltpu.SemaphoreType.DMA((ITERS,)),
    ]
    return kernel, scratch


def shards(n_row, n_col, source_embed, target_embed, source_mass, target_mass, tile_list, tile_counts):
    cells = source_embed.shape[1]
    dim = source_embed.shape[0] * n_col
    blocks = cells // LANES
    kernel, scratch = make_kernel(n_row, n_col, RING_Y, cells, dim, tile_list.shape[3])
    side = pltpu.VMEM((blocks, LANES), jnp.float32)
    source_side, target_side = pl.pallas_call(
        kernel,
        out_shape=(side, side),
        in_specs=[pl.BlockSpec(memory_space=pl.ANY)] * 6,
        out_specs=[pl.BlockSpec(memory_space=pltpu.VMEM)] * 2,
        scratch_shapes=scratch,
        compiler_params=pltpu.CompilerParams(collective_id=0, has_side_effects=True),
        name="sinkhorn",
    )(
        source_embed,
        target_embed,
        source_mass.reshape(blocks, LANES),
        target_mass.reshape(blocks, LANES),
        tile_list,
        tile_counts,
    )
    unit = entropic / log2e
    return (source_side * unit).reshape(cells), (target_side * unit).reshape(cells)


def solution(mesh):
    in_specs = (
        P("col", "row"),
        P("row", "col"),
        P("row"),
        P("col"),
        P("row", "col", None, None),
        P("row", "col"),
    )
    out_specs = (P("row"), P("col"))
    body = functools.partial(shards, mesh.shape["row"], mesh.shape["col"])
    return jax.shard_map(body, mesh=mesh, in_specs=in_specs, out_specs=out_specs, check_vma=False)
```

```python
import functools
import math

import jax
import jax.numpy as jnp
from jax import lax
from jax.experimental import pallas as pl
from jax.experimental.pallas import tpu as pltpu
from jax.sharding import PartitionSpec as P

TILE = 256
ITERS = 3
RING_Y = 8
CORES = 2
SPAN = 64
UNROLL = 4
HALVES = 2

entropic = 0.1
dead_cost = 1e30
log2e = math.log2(math.e)
MESH = pl.DeviceIdType.MESH
LANES = 128


def ring_offsets(size):
    return sorted(range(1, size), key=lambda k: -min(k, size - k))


def wait_bytes(ref, sem):
    pltpu.make_async_copy(ref, ref, sem).wait()


def split_three(x):
    high = x.astype(jnp.bfloat16)
    rest = x - high.astype(jnp.float32)
    middle = rest.astype(jnp.bfloat16)
    low = (rest - middle.astype(jnp.float32)).astype(jnp.bfloat16)
    return high, middle, low


def combine(parts):
    highest = functools.reduce(jnp.maximum, parts)
    total = functools.reduce(jnp.add, [jnp.exp2(part - highest) for part in parts])
    return highest + jnp.log2(total)


def make_kernel(n_row, n_col, ring_y, cells, dim, slot_count):
    ring_x = n_col // ring_y
    ring_z = n_row // CORES
    blocks = cells // LANES
    src_rows = dim // n_col
    tgt_rows = dim // n_row
    per = max(src_rows, tgt_rows)
    steps = dim // per
    part = blocks // HALVES
    src_size = src_rows * blocks
    tgt_size = tgt_rows * blocks
    tiles = cells // TILE
    x_offsets = ring_offsets(ring_x)
    y_offsets = ring_offsets(ring_y)
    z_offsets = [(0, 1)] + [(dz, dc) for dz in range(1, ring_z) for dc in range(CORES)]
    z_offsets.sort(key=lambda o: -min(o[0], ring_z - o[0]))
    def reach_of(dx, dy):
        return min(dx, ring_x - dx) + min(dy, ring_y - dy)

    plane_offsets = [(dx, dy) for dx in range(ring_x) for dy in range(ring_y) if dx or dy]
    plane_offsets.sort(key=lambda o: -reach_of(*o))
    plane_far = sum(2 * reach_of(*o) > ring_x // 2 + ring_y // 2 for o in plane_offsets)
    plane_near = len(plane_offsets) - plane_far
    z_far = sum(2 * min(dz, ring_z - dz) > ring_z // 2 for dz, dc in z_offsets)
    z_near = len(z_offsets) - z_far

    def kernel(
        src_hbm,
        tgt_hbm,
        smass_hbm,
        tmass_hbm,
        list_hbm,
        count_hbm,
        source_out,
        target_out,
        src_ref,
        tgt_ref,
        smass_ref,
        tmass_ref,
        list_ref,
        count_ref,
        gsrc,
        gtgt,
        left,
        right,
        cost,
        cost_t,
        penalty,
        spread,
        state,
        part_row,
        part_col,
        far_row,
        far_col,
        near_row,
        near_col,
        load_sem,
        gather_send,
        y_recv,
        z_recv,
        x_recv,
        row_send,
        col_send,
        far_row_recv,
        far_col_recv,
        near_row_recv,
        near_col_recv,
    ):
        row = lax.axis_index("row")
        col = lax.axis_index("col")
        x, y = col // ring_y, col % ring_y
        z, core = row // CORES, row % CORES
        x_peers = [(row, (x + dx) % ring_x * ring_y + y) for dx in x_offsets]
        y_peers = [(row, x * ring_y + (y + dy) % ring_y) for dy in y_offsets]
        z_peers = [((z + dz) % ring_z * CORES + (core + dc) % CORES, col) for dz, dc in z_offsets]
        plane_peers = [
            (row, (x + dx) % ring_x * ring_y + (y + dy) % ring_y) for dx, dy in plane_offsets
        ]

        loads = [
            pltpu.make_async_copy(hbm, ref, load_sem.at[k])
            for k, (hbm, ref) in enumerate(
                [
                    (src_hbm, src_ref),
                    (tgt_hbm, tgt_ref),
                    (smass_hbm, smass_ref),
                    (tmass_hbm, tmass_ref),
                    (list_hbm, list_ref),
                    (count_hbm, count_ref),
                ]
            )
        ]
        for load in loads:
            load.start()
        barrier = pltpu.get_barrier_semaphore()
        greeted = y_peers + z_peers + x_peers
        for peer in greeted:
            pl.semaphore_signal(barrier, inc=1, device_id=peer, device_id_type=MESH)

        def src_chunk(owner):
            return gsrc.at[pl.ds(pl.multiple_of(owner * src_size, src_size), src_size)]

        def tgt_chunk(owner):
            return gtgt.at[pl.ds(pl.multiple_of(owner * tgt_size, tgt_size), tgt_size)]

        own_src = src_chunk(col)
        own_tgt = tgt_chunk(row)
        for load in loads:
            load.wait()
        for b in range(blocks):
            own_src[b * src_rows : (b + 1) * src_rows, :] = src_ref[:, b * LANES : (b + 1) * LANES]
            own_tgt[b * tgt_rows : (b + 1) * tgt_rows, :] = tgt_ref[:, b * LANES : (b + 1) * LANES]

        pl.semaphore_wait(barrier, len(greeted))

        def send(src, dst, send_sem, recv_sem, peer):
            pltpu.make_async_remote_copy(
                src_ref=src,
                dst_ref=dst,
                send_sem=send_sem,
                recv_sem=recv_sem,
                device_id=peer,
                device_id_type=MESH,
            ).start()

        for peer in y_peers:
            send(own_src, own_src, gather_send.at[0], y_recv, peer)
        for peer in z_peers:
            send(own_tgt, own_tgt, gather_send.at[1], z_recv, peer)

        slots = list_ref[0, 0]
        tile_ids = (slots[0:1, :] - row * tiles) * tiles + (slots[1:2, :] - col * tiles)
        live = lax.broadcasted_iota(jnp.int32, (1, slot_count), 1) < count_ref[...]
        tile_ids = jnp.where(live, tile_ids, -1)
        wanted = lax.broadcasted_iota(jnp.int32, (tiles * tiles * 8, slot_count), 0) // 8
        hits = jnp.where(wanted == tile_ids, 1.0, 0.0)
        found = jnp.max(hits, axis=1, keepdims=True)
        penalty[...] = jnp.broadcast_to(jnp.where(found > 0.5, 0.0, dead_cost), penalty.shape)

        unit = log2e / (entropic * 2.0 * dim)

        def load_features(ref, b, rows):
            found = []
            for q in range(per):
                start = q // rows * (blocks * rows) + b * rows + q % rows
                found.append(ref[pl.Slice(start, steps, per * blocks), :])
            return jnp.concatenate(found, axis=0)

        depth = left.shape[0]
        extra_rows = depth - 6 * dim

        def operands(gathered, out, rows, scale, is_left):
            for b in range(blocks):
                lanes = slice(b * LANES, (b + 1) * LANES)
                values = load_features(gathered, b, rows)
                norms = jnp.sum(values * values, axis=0, keepdims=True) * unit
                high, middle, low = split_three(values * scale if scale != 1.0 else values)
                order = (high, high, middle, middle, high, low)
                if not is_left:
                    order = (high, middle, high, middle, low, high)
                for k, term in enumerate(order):
                    out[k * dim : (k + 1) * dim, lanes] = term
                parts = [p.astype(jnp.float32) for p in split_three(norms)]
                one = jnp.ones((1, LANES), jnp.float32)
                pieces = parts + [one] * 3 if is_left else [one] * 3 + parts
                index = lax.broadcasted_iota(jnp.int32, (extra_rows, LANES), 0)
                extra = jnp.zeros((extra_rows, LANES), jnp.float32)
                for k, piece in enumerate(pieces):
                    extra = jnp.where(index == k, piece, extra)
                out[6 * dim :, lanes] = extra.astype(jnp.bfloat16)

        def fill(dst, lhs, rhs, major, minor):
            def one_row(rb, carry):
                rows = pl.ds(pl.multiple_of(rb * TILE, TILE), TILE)
                block = lhs[:, rows]
                for cb in range(tiles):
                    product = lax.dot_general(
                        block,
                        rhs[:, cb * TILE : (cb + 1) * TILE],
                        (((0,), (0,)), ((), ())),
                        preferred_element_type=jnp.float32,
                    )
                    tile = rb * major + cb * minor
                    extra = penalty[pl.ds(pl.multiple_of(tile * 8, 8), 8), :]
                    dst[rows, cb * TILE : (cb + 1) * TILE] = product + jnp.broadcast_to(
                        extra[0:1, 0:1], product.shape
                    )
                return carry

            lax.fori_loop(0, tiles, one_row, 0)

        def spread_half(potential, half):
            turned = potential.T
            for b in range(part):
                start = (half * part + b) * LANES
                spread[start : start + LANES, :] = jnp.broadcast_to(
                    turned[:, b : b + 1], (LANES, LANES)
                )

        def sweep(costs, half, chosen, pairs):
            reach = cells // HALVES

            def step(g, carry):
                rows = pl.ds(pl.multiple_of(half * reach + g * SPAN, SPAN), SPAN)
                shift = spread[rows, :]
                result = []
                for b, (highest, total) in zip(chosen, carry):
                    scores = shift - costs[rows, b * LANES : (b + 1) * LANES]
                    scores = scores.reshape(SPAN // 8, 8, LANES)
                    raised = jnp.maximum(highest, jnp.max(scores, axis=0))
                    fresh = jnp.sum(jnp.exp2(scores - raised[None]), axis=0)
                    result.append((raised, total * jnp.exp2(highest - raised) + fresh))
                return tuple(result)

            return lax.fori_loop(0, reach // SPAN, step, tuple(pairs), unroll=UNROLL)

        def finish(pairs):
            index = lax.broadcasted_iota(jnp.int32, (part, LANES), 0)
            lse_max = jnp.zeros((part, LANES), jnp.float32)
            lse_sum = jnp.ones((part, LANES), jnp.float32)
            for b, (highest, total) in enumerate(pairs):
                top = jnp.max(highest, axis=0, keepdims=True)
                total = jnp.sum(total * jnp.exp2(highest - top), axis=0, keepdims=True)
                lse_max = jnp.where(index == b, top, lse_max)
                lse_sum = jnp.where(index == b, total, lse_sum)
            return lse_max + jnp.log2(lse_sum)

        def open_pass(costs, potential):
            spread_half(potential, 0)
            low = jnp.full((8, LANES), -3e38, jnp.float32)
            none = jnp.zeros((8, LANES), jnp.float32)
            pairs = sweep(costs, 0, range(blocks), [(low, none)] * blocks)
            for b, (highest, total) in enumerate(pairs):
                state[0, b] = highest
                state[1, b] = total

        def close_pass(costs, potential, emit):
            spread_half(potential, 1)
            for half in range(HALVES):
                chosen = range(half * part, (half + 1) * part)
                pairs = sweep(costs, 1, chosen, [(state[0, b], state[1, b]) for b in chosen])
                emit(half, finish(pairs))

        def merged(own, far, near, turn, half):
            parts = [far[turn, half, k] for k in range(far.shape[2])]
            parts += [near[turn, k, half] for k in range(near.shape[1])]
            return combine([own[turn, half]] + parts)

        def emit_to(peers, own, far, near, sends, far_recv, near_recv, turn, half, lse):
            own[turn, half] = lse
            far_count = far.shape[2]
            for k, peer in enumerate(peers[:far_count]):
                send(
                    own.at[turn, half],
                    far.at[turn, half, k],
                    sends.at[0],
                    far_recv.at[turn, half],
                    peer,
                )
            if half == HALVES - 1:
                for k, peer in enumerate(peers[far_count:]):
                    send(own.at[turn], near.at[turn, k], sends.at[1], near_recv.at[turn], peer)

        wait_bytes(gsrc.at[pl.ds(0, len(y_peers) * src_size)], y_recv)
        group = ring_y * src_size
        own_group = gsrc.at[pl.ds(pl.multiple_of(x * group, group), group)]
        for peer in x_peers:
            send(own_group, own_group, gather_send.at[2], x_recv, peer)
        wait_bytes(gtgt.at[pl.ds(0, len(z_peers) * tgt_size)], z_recv)
        operands(gtgt, right, tgt_rows, 1.0, False)
        wait_bytes(gsrc.at[pl.ds(0, len(x_peers) * ring_y * src_size)], x_recv)
        operands(gsrc, left, src_rows, -2.0 * unit, True)
        fill(cost_t, right, left, 1, tiles)

        source_mass = [smass_ref[h * part : (h + 1) * part, :] * log2e for h in range(HALVES)]
        target_mass = [tmass_ref[h * part : (h + 1) * part, :] * log2e for h in range(HALVES)]
        zero = jnp.zeros((part, LANES), jnp.float32)
        open_pass(cost_t, zero)

        def iterate(turn, target_late):
            emit_row = functools.partial(
                emit_to,
                plane_peers,
                part_row,
                far_row,
                near_row,
                row_send,
                far_row_recv,
                near_row_recv,
                turn,
            )
            emit_col = functools.partial(
                emit_to,
                z_peers,
                part_col,
                far_col,
                near_col,
                col_send,
                far_col_recv,
                near_col_recv,
                turn,
            )

            def source_half(half):
                wait_bytes(far_row.at[turn, half], far_row_recv.at[turn, half])
                if half == 0:
                    wait_bytes(near_row.at[turn], near_row_recv.at[turn])
                lse = merged(part_row, far_row, near_row, turn, half)
                source_out[half * part : (half + 1) * part, :] = source_mass[half] - lse
                return source_mass[half] - lse

            def target_half(half):
                wait_bytes(far_col.at[turn, half], far_col_recv.at[turn, half])
                if half == 0:
                    wait_bytes(near_col.at[turn], near_col_recv.at[turn])
                lse = merged(part_col, far_col, near_col, turn, half)
                target_out[half * part : (half + 1) * part, :] = target_mass[half] - lse
                return target_mass[half] - lse

            close_pass(cost_t, target_late, emit_row)

            @pl.when(turn == 0)
            def fill_cost():
                fill(cost, left, right, tiles, 1)

            open_pass(cost, source_half(0))
            close_pass(cost, source_half(1), emit_col)
            target_early = target_half(0)

            @pl.when(turn < ITERS - 1)
            def next_pass():
                open_pass(cost_t, target_early)

            return target_half(1)

        lax.fori_loop(0, ITERS, iterate, zero)

        wait_bytes(gsrc.at[pl.ds(0, len(y_peers) * src_size)], gather_send.at[0])
        wait_bytes(gtgt.at[pl.ds(0, len(z_peers) * tgt_size)], gather_send.at[1])
        wait_bytes(gsrc.at[pl.ds(0, len(x_peers) * ring_y * src_size)], gather_send.at[2])
        wait_bytes(far_row, row_send.at[0])
        wait_bytes(near_row, row_send.at[1])
        wait_bytes(far_col, col_send.at[0])
        wait_bytes(near_col, col_send.at[1])

    def far_slots(count):
        return pltpu.VMEM((ITERS, HALVES, count, part, LANES), jnp.float32)

    def near_slots(count):
        return pltpu.VMEM((ITERS, count, HALVES, part, LANES), jnp.float32)

    depth = 6 * dim + LANES
    scratch = [
        pltpu.VMEM((src_rows, cells), jnp.float32),
        pltpu.VMEM((tgt_rows, cells), jnp.float32),
        pltpu.VMEM((blocks, LANES), jnp.float32),
        pltpu.VMEM((blocks, LANES), jnp.float32),
        pltpu.VMEM((1, 1, 2, slot_count), jnp.int32),
        pltpu.VMEM((1, 1), jnp.int32),
        pltpu.VMEM((dim * blocks, LANES), jnp.float32),
        pltpu.VMEM((dim * blocks, LANES), jnp.float32),
        pltpu.VMEM((depth, cells), jnp.bfloat16),
        pltpu.VMEM((depth, cells), jnp.bfloat16),
        pltpu.VMEM((cells, cells), jnp.float32),
        pltpu.VMEM((cells, cells), jnp.float32),
        pltpu.VMEM((tiles * tiles * 8, LANES), jnp.float32),
        pltpu.VMEM((cells, LANES), jnp.float32),
        pltpu.VMEM((2, blocks, 8, LANES), jnp.float32),
        pltpu.VMEM((ITERS, HALVES, part, LANES), jnp.float32),
        pltpu.VMEM((ITERS, HALVES, part, LANES), jnp.float32),
        far_slots(plane_far),
        far_slots(z_far),
        near_slots(plane_near),
        near_slots(z_near),
        pltpu.SemaphoreType.DMA((6,)),
        pltpu.SemaphoreType.DMA((3,)),
        pltpu.SemaphoreType.DMA,
        pltpu.SemaphoreType.DMA,
        pltpu.SemaphoreType.DMA,
        pltpu.SemaphoreType.DMA((2,)),
        pltpu.SemaphoreType.DMA((2,)),
        pltpu.SemaphoreType.DMA((ITERS, HALVES)),
        pltpu.SemaphoreType.DMA((ITERS, HALVES)),
        pltpu.SemaphoreType.DMA((ITERS,)),
        pltpu.SemaphoreType.DMA((ITERS,)),
    ]
    return kernel, scratch


def shards(n_row, n_col, source_embed, target_embed, source_mass, target_mass, tile_list, tile_counts):
    cells = source_embed.shape[1]
    dim = source_embed.shape[0] * n_col
    blocks = cells // LANES
    kernel, scratch = make_kernel(n_row, n_col, RING_Y, cells, dim, tile_list.shape[3])
    side = pltpu.VMEM((blocks, LANES), jnp.float32)
    source_side, target_side = pl.pallas_call(
        kernel,
        out_shape=(side, side),
        in_specs=[pl.BlockSpec(memory_space=pl.ANY)] * 6,
        out_specs=[pl.BlockSpec(memory_space=pltpu.VMEM)] * 2,
        scratch_shapes=scratch,
        compiler_params=pltpu.CompilerParams(collective_id=0, has_side_effects=True),
        name="sinkhorn",
    )(
        source_embed,
        target_embed,
        source_mass.reshape(blocks, LANES),
        target_mass.reshape(blocks, LANES),
        tile_list,
        tile_counts,
    )
    unit = entropic / log2e
    return (source_side * unit).reshape(cells), (target_side * unit).reshape(cells)


def solution(mesh):
    in_specs = (
        P("col", "row"),
        P("row", "col"),
        P("row"),
        P("col"),
        P("row", "col", None, None),
        P("row", "col"),
    )
    out_specs = (P("row"), P("col"))
    body = functools.partial(shards, mesh.shape["row"], mesh.shape["col"])
    return jax.shard_map(body, mesh=mesh, in_specs=in_specs, out_specs=out_specs, check_vma=False)
```

```python
import functools
import math

import jax
import jax.numpy as jnp
from jax import lax
from jax.experimental import pallas as pl
from jax.experimental.pallas import tpu as pltpu
from jax.sharding import PartitionSpec as P

TILE = 256
ITERS = 3
RING_Y = 8
CORES = 2
SPAN = 64
UNROLL = 8
HALVES = 2

entropic = 0.1
dead_cost = 1e30
log2e = math.log2(math.e)
MESH = pl.DeviceIdType.MESH
LANES = 128


def ring_offsets(size):
    return sorted(range(1, size), key=lambda k: -min(k, size - k))


def wait_bytes(ref, sem):
    pltpu.make_async_copy(ref, ref, sem).wait()


def split_three(x):
    high = x.astype(jnp.bfloat16)
    rest = x - high.astype(jnp.float32)
    middle = rest.astype(jnp.bfloat16)
    low = (rest - middle.astype(jnp.float32)).astype(jnp.bfloat16)
    return high, middle, low


def combine(parts):
    highest = functools.reduce(jnp.maximum, parts)
    total = functools.reduce(jnp.add, [jnp.exp2(part - highest) for part in parts])
    return highest + jnp.log2(total)


def make_kernel(n_row, n_col, ring_y, cells, dim, slot_count):
    ring_x = n_col // ring_y
    ring_z = n_row // CORES
    blocks = cells // LANES
    src_rows = dim // n_col
    tgt_rows = dim // n_row
    per = max(src_rows, tgt_rows)
    steps = dim // per
    part = blocks // HALVES
    src_size = src_rows * blocks
    tgt_size = tgt_rows * blocks
    tiles = cells // TILE
    x_offsets = ring_offsets(ring_x)
    y_offsets = ring_offsets(ring_y)
    z_offsets = [(0, 1)] + [(dz, dc) for dz in range(1, ring_z) for dc in range(CORES)]
    z_offsets.sort(key=lambda o: -min(o[0], ring_z - o[0]))
    def reach_of(dx, dy):
        return min(dx, ring_x - dx) + min(dy, ring_y - dy)

    plane_offsets = [(dx, dy) for dx in range(ring_x) for dy in range(ring_y) if dx or dy]
    plane_offsets.sort(key=lambda o: -reach_of(*o))
    plane_far = sum(2 * reach_of(*o) > ring_x // 2 + ring_y // 2 for o in plane_offsets)
    plane_near = len(plane_offsets) - plane_far
    z_far = sum(2 * min(dz, ring_z - dz) > ring_z // 2 for dz, dc in z_offsets)
    z_near = len(z_offsets) - z_far

    def kernel(
        src_hbm,
        tgt_hbm,
        smass_hbm,
        tmass_hbm,
        list_hbm,
        count_hbm,
        source_out,
        target_out,
        src_ref,
        tgt_ref,
        smass_ref,
        tmass_ref,
        list_ref,
        count_ref,
        gsrc,
        gtgt,
        left,
        right,
        cost,
        cost_t,
        penalty,
        spread,
        state,
        part_row,
        part_col,
        far_row,
        far_col,
        near_row,
        near_col,
        load_sem,
        gather_send,
        y_recv,
        z_recv,
        x_recv,
        row_send,
        col_send,
        far_row_recv,
        far_col_recv,
        near_row_recv,
        near_col_recv,
    ):
        row = lax.axis_index("row")
        col = lax.axis_index("col")
        x, y = col // ring_y, col % ring_y
        z, core = row // CORES, row % CORES
        x_peers = [(row, (x + dx) % ring_x * ring_y + y) for dx in x_offsets]
        y_peers = [(row, x * ring_y + (y + dy) % ring_y) for dy in y_offsets]
        z_peers = [((z + dz) % ring_z * CORES + (core + dc) % CORES, col) for dz, dc in z_offsets]
        plane_peers = [
            (row, (x + dx) % ring_x * ring_y + (y + dy) % ring_y) for dx, dy in plane_offsets
        ]

        loads = [
            pltpu.make_async_copy(hbm, ref, load_sem.at[k])
            for k, (hbm, ref) in enumerate(
                [
                    (src_hbm, src_ref),
                    (tgt_hbm, tgt_ref),
                    (smass_hbm, smass_ref),
                    (tmass_hbm, tmass_ref),
                    (list_hbm, list_ref),
                    (count_hbm, count_ref),
                ]
            )
        ]
        for load in loads:
            load.start()
        barrier = pltpu.get_barrier_semaphore()
        greeted = y_peers + z_peers + x_peers
        for peer in greeted:
            pl.semaphore_signal(barrier, inc=1, device_id=peer, device_id_type=MESH)

        def src_chunk(owner):
            return gsrc.at[pl.ds(pl.multiple_of(owner * src_size, src_size), src_size)]

        def tgt_chunk(owner):
            return gtgt.at[pl.ds(pl.multiple_of(owner * tgt_size, tgt_size), tgt_size)]

        own_src = src_chunk(col)
        own_tgt = tgt_chunk(row)
        for load in loads:
            load.wait()
        for b in range(blocks):
            own_src[b * src_rows : (b + 1) * src_rows, :] = src_ref[:, b * LANES : (b + 1) * LANES]
            own_tgt[b * tgt_rows : (b + 1) * tgt_rows, :] = tgt_ref[:, b * LANES : (b + 1) * LANES]

        pl.semaphore_wait(barrier, len(greeted))

        def send(src, dst, send_sem, recv_sem, peer):
            pltpu.make_async_remote_copy(
                src_ref=src,
                dst_ref=dst,
                send_sem=send_sem,
                recv_sem=recv_sem,
                device_id=peer,
                device_id_type=MESH,
            ).start()

        for peer in y_peers:
            send(own_src, own_src, gather_send.at[0], y_recv, peer)
        for peer in z_peers:
            send(own_tgt, own_tgt, gather_send.at[1], z_recv, peer)

        slots = list_ref[0, 0]
        tile_ids = (slots[0:1, :] - row * tiles) * tiles + (slots[1:2, :] - col * tiles)
        live = lax.broadcasted_iota(jnp.int32, (1, slot_count), 1) < count_ref[...]
        tile_ids = jnp.where(live, tile_ids, -1)
        wanted = lax.broadcasted_iota(jnp.int32, (tiles * tiles * 8, slot_count), 0) // 8
        hits = jnp.where(wanted == tile_ids, 1.0, 0.0)
        found = jnp.max(hits, axis=1, keepdims=True)
        penalty[...] = jnp.broadcast_to(jnp.where(found > 0.5, 0.0, dead_cost), penalty.shape)

        unit = log2e / (entropic * 2.0 * dim)

        def load_features(ref, b, rows):
            found = []
            for q in range(per):
                start = q // rows * (blocks * rows) + b * rows + q % rows
                found.append(ref[pl.Slice(start, steps, per * blocks), :])
            return jnp.concatenate(found, axis=0)

        depth = left.shape[0]
        extra_rows = depth - 6 * dim

        def operands(gathered, out, rows, scale, is_left):
            for b in range(blocks):
                lanes = slice(b * LANES, (b + 1) * LANES)
                values = load_features(gathered, b, rows)
                norms = jnp.sum(values * values, axis=0, keepdims=True) * unit
                high, middle, low = split_three(values * scale if scale != 1.0 else values)
                order = (high, high, middle, middle, high, low)
                if not is_left:
                    order = (high, middle, high, middle, low, high)
                for k, term in enumerate(order):
                    out[k * dim : (k + 1) * dim, lanes] = term
                parts = [p.astype(jnp.float32) for p in split_three(norms)]
                one = jnp.ones((1, LANES), jnp.float32)
                pieces = parts + [one] * 3 if is_left else [one] * 3 + parts
                index = lax.broadcasted_iota(jnp.int32, (extra_rows, LANES), 0)
                extra = jnp.zeros((extra_rows, LANES), jnp.float32)
                for k, piece in enumerate(pieces):
                    extra = jnp.where(index == k, piece, extra)
                out[6 * dim :, lanes] = extra.astype(jnp.bfloat16)

        def fill(dst, lhs, rhs, major, minor):
            def one_row(rb, carry):
                rows = pl.ds(pl.multiple_of(rb * TILE, TILE), TILE)
                block = lhs[:, rows]
                for cb in range(tiles):
                    product = lax.dot_general(
                        block,
                        rhs[:, cb * TILE : (cb + 1) * TILE],
                        (((0,), (0,)), ((), ())),
                        preferred_element_type=jnp.float32,
                    )
                    tile = rb * major + cb * minor
                    extra = penalty[pl.ds(pl.multiple_of(tile * 8, 8), 8), :]
                    dst[rows, cb * TILE : (cb + 1) * TILE] = product + jnp.broadcast_to(
                        extra[0:1, 0:1], product.shape
                    )
                return carry

            lax.fori_loop(0, tiles, one_row, 0)

        def spread_half(potential, half):
            turned = potential.T
            for b in range(part):
                start = (half * part + b) * LANES
                spread[start : start + LANES, :] = jnp.broadcast_to(
                    turned[:, b : b + 1], (LANES, LANES)
                )

        def sweep(costs, half, chosen, pairs):
            reach = cells // HALVES

            def step(g, carry):
                rows = pl.ds(pl.multiple_of(half * reach + g * SPAN, SPAN), SPAN)
                shift = spread[rows, :]
                result = []
                for b, (highest, total) in zip(chosen, carry):
                    scores = shift - costs[rows, b * LANES : (b + 1) * LANES]
                    scores = scores.reshape(SPAN // 8, 8, LANES)
                    raised = jnp.maximum(highest, jnp.max(scores, axis=0))
                    fresh = jnp.sum(jnp.exp2(scores - raised[None]), axis=0)
                    result.append((raised, total * jnp.exp2(highest - raised) + fresh))
                return tuple(result)

            return lax.fori_loop(0, reach // SPAN, step, tuple(pairs), unroll=UNROLL)

        def finish(pairs):
            index = lax.broadcasted_iota(jnp.int32, (part, LANES), 0)
            lse_max = jnp.zeros((part, LANES), jnp.float32)
            lse_sum = jnp.ones((part, LANES), jnp.float32)
            for b, (highest, total) in enumerate(pairs):
                top = jnp.max(highest, axis=0, keepdims=True)
                total = jnp.sum(total * jnp.exp2(highest - top), axis=0, keepdims=True)
                lse_max = jnp.where(index == b, top, lse_max)
                lse_sum = jnp.where(index == b, total, lse_sum)
            return lse_max + jnp.log2(lse_sum)

        def open_pass(costs, potential):
            spread_half(potential, 0)
            low = jnp.full((8, LANES), -3e38, jnp.float32)
            none = jnp.zeros((8, LANES), jnp.float32)
            pairs = sweep(costs, 0, range(blocks), [(low, none)] * blocks)
            for b, (highest, total) in enumerate(pairs):
                state[0, b] = highest
                state[1, b] = total

        def close_pass(costs, potential, emit):
            spread_half(potential, 1)
            for half in range(HALVES):
                chosen = range(half * part, (half + 1) * part)
                pairs = sweep(costs, 1, chosen, [(state[0, b], state[1, b]) for b in chosen])
                emit(half, finish(pairs))

        def merged(own, far, near, turn, half):
            parts = [far[turn, half, k] for k in range(far.shape[2])]
            parts += [near[turn, k, half] for k in range(near.shape[1])]
            return combine([own[turn, half]] + parts)

        def emit_to(peers, own, far, near, sends, far_recv, near_recv, turn, half, lse):
            own[turn, half] = lse
            far_count = far.shape[2]
            for k, peer in enumerate(peers[:far_count]):
                send(
                    own.at[turn, half],
                    far.at[turn, half, k],
                    sends.at[0],
                    far_recv.at[turn, half],
                    peer,
                )
            if half == HALVES - 1:
                for k, peer in enumerate(peers[far_count:]):
                    send(own.at[turn], near.at[turn, k], sends.at[1], near_recv.at[turn], peer)

        wait_bytes(gsrc.at[pl.ds(0, len(y_peers) * src_size)], y_recv)
        group = ring_y * src_size
        own_group = gsrc.at[pl.ds(pl.multiple_of(x * group, group), group)]
        for peer in x_peers:
            send(own_group, own_group, gather_send.at[2], x_recv, peer)
        wait_bytes(gtgt.at[pl.ds(0, len(z_peers) * tgt_size)], z_recv)
        operands(gtgt, right, tgt_rows, 1.0, False)
        wait_bytes(gsrc.at[pl.ds(0, len(x_peers) * ring_y * src_size)], x_recv)
        operands(gsrc, left, src_rows, -2.0 * unit, True)
        fill(cost_t, right, left, 1, tiles)

        source_mass = [smass_ref[h * part : (h + 1) * part, :] * log2e for h in range(HALVES)]
        target_mass = [tmass_ref[h * part : (h + 1) * part, :] * log2e for h in range(HALVES)]
        zero = jnp.zeros((part, LANES), jnp.float32)
        open_pass(cost_t, zero)

        def iterate(turn, target_late):
            emit_row = functools.partial(
                emit_to,
                plane_peers,
                part_row,
                far_row,
                near_row,
                row_send,
                far_row_recv,
                near_row_recv,
                turn,
            )
            emit_col = functools.partial(
                emit_to,
                z_peers,
                part_col,
                far_col,
                near_col,
                col_send,
                far_col_recv,
                near_col_recv,
                turn,
            )

            def source_half(half):
                wait_bytes(far_row.at[turn, half], far_row_recv.at[turn, half])
                if half == 0:
                    wait_bytes(near_row.at[turn], near_row_recv.at[turn])
                lse = merged(part_row, far_row, near_row, turn, half)
                source_out[half * part : (half + 1) * part, :] = source_mass[half] - lse
                return source_mass[half] - lse

            def target_half(half):
                wait_bytes(far_col.at[turn, half], far_col_recv.at[turn, half])
                if half == 0:
                    wait_bytes(near_col.at[turn], near_col_recv.at[turn])
                lse = merged(part_col, far_col, near_col, turn, half)
                target_out[half * part : (half + 1) * part, :] = target_mass[half] - lse
                return target_mass[half] - lse

            close_pass(cost_t, target_late, emit_row)

            @pl.when(turn == 0)
            def fill_cost():
                fill(cost, left, right, tiles, 1)

            open_pass(cost, source_half(0))
            close_pass(cost, source_half(1), emit_col)
            target_early = target_half(0)

            @pl.when(turn < ITERS - 1)
            def next_pass():
                open_pass(cost_t, target_early)

            return target_half(1)

        lax.fori_loop(0, ITERS, iterate, zero)

        wait_bytes(gsrc.at[pl.ds(0, len(y_peers) * src_size)], gather_send.at[0])
        wait_bytes(gtgt.at[pl.ds(0, len(z_peers) * tgt_size)], gather_send.at[1])
        wait_bytes(gsrc.at[pl.ds(0, len(x_peers) * ring_y * src_size)], gather_send.at[2])
        wait_bytes(far_row, row_send.at[0])
        wait_bytes(near_row, row_send.at[1])
        wait_bytes(far_col, col_send.at[0])
        wait_bytes(near_col, col_send.at[1])

    def far_slots(count):
        return pltpu.VMEM((ITERS, HALVES, count, part, LANES), jnp.float32)

    def near_slots(count):
        return pltpu.VMEM((ITERS, count, HALVES, part, LANES), jnp.float32)

    depth = 6 * dim + LANES
    scratch = [
        pltpu.VMEM((src_rows, cells), jnp.float32),
        pltpu.VMEM((tgt_rows, cells), jnp.float32),
        pltpu.VMEM((blocks, LANES), jnp.float32),
        pltpu.VMEM((blocks, LANES), jnp.float32),
        pltpu.VMEM((1, 1, 2, slot_count), jnp.int32),
        pltpu.VMEM((1, 1), jnp.int32),
        pltpu.VMEM((dim * blocks, LANES), jnp.float32),
        pltpu.VMEM((dim * blocks, LANES), jnp.float32),
        pltpu.VMEM((depth, cells), jnp.bfloat16),
        pltpu.VMEM((depth, cells), jnp.bfloat16),
        pltpu.VMEM((cells, cells), jnp.float32),
        pltpu.VMEM((cells, cells), jnp.float32),
        pltpu.VMEM((tiles * tiles * 8, LANES), jnp.float32),
        pltpu.VMEM((cells, LANES), jnp.float32),
        pltpu.VMEM((2, blocks, 8, LANES), jnp.float32),
        pltpu.VMEM((ITERS, HALVES, part, LANES), jnp.float32),
        pltpu.VMEM((ITERS, HALVES, part, LANES), jnp.float32),
        far_slots(plane_far),
        far_slots(z_far),
        near_slots(plane_near),
        near_slots(z_near),
        pltpu.SemaphoreType.DMA((6,)),
        pltpu.SemaphoreType.DMA((3,)),
        pltpu.SemaphoreType.DMA,
        pltpu.SemaphoreType.DMA,
        pltpu.SemaphoreType.DMA,
        pltpu.SemaphoreType.DMA((2,)),
        pltpu.SemaphoreType.DMA((2,)),
        pltpu.SemaphoreType.DMA((ITERS, HALVES)),
        pltpu.SemaphoreType.DMA((ITERS, HALVES)),
        pltpu.SemaphoreType.DMA((ITERS,)),
        pltpu.SemaphoreType.DMA((ITERS,)),
    ]
    return kernel, scratch


def shards(n_row, n_col, source_embed, target_embed, source_mass, target_mass, tile_list, tile_counts):
    cells = source_embed.shape[1]
    dim = source_embed.shape[0] * n_col
    blocks = cells // LANES
    kernel, scratch = make_kernel(n_row, n_col, RING_Y, cells, dim, tile_list.shape[3])
    side = pltpu.VMEM((blocks, LANES), jnp.float32)
    source_side, target_side = pl.pallas_call(
        kernel,
        out_shape=(side, side),
        in_specs=[pl.BlockSpec(memory_space=pl.ANY)] * 6,
        out_specs=[pl.BlockSpec(memory_space=pltpu.VMEM)] * 2,
        scratch_shapes=scratch,
        compiler_params=pltpu.CompilerParams(collective_id=0, has_side_effects=True),
        name="sinkhorn",
    )(
        source_embed,
        target_embed,
        source_mass.reshape(blocks, LANES),
        target_mass.reshape(blocks, LANES),
        tile_list,
        tile_counts,
    )
    unit = entropic / log2e
    return (source_side * unit).reshape(cells), (target_side * unit).reshape(cells)


def solution(mesh):
    in_specs = (
        P("col", "row"),
        P("row", "col"),
        P("row"),
        P("col"),
        P("row", "col", None, None),
        P("row", "col"),
    )
    out_specs = (P("row"), P("col"))
    body = functools.partial(shards, mesh.shape["row"], mesh.shape["col"])
    return jax.shard_map(body, mesh=mesh, in_specs=in_specs, out_specs=out_specs, check_vma=False)
```
